32 devices in a mesh: groups: 2 (over x), tile: 16 (over z, y, core).
Axes of the slice: x: 2, y: 2, z: 4, core: 2. Of those that a mesh axis runs over, the one named last changes fastest.
Arguments:
- queries: bfloat16 [2048, 4096], P(('groups', 'tile')), parts along dimension 0, may hold values from -8 to 8
- key_rows: bfloat16 [2048, 4096], P(('groups', 'tile')), parts along dimension 0, may hold values from -8 to 8
- values: bfloat16 [2048, 4096], P(('groups', 'tile')), parts along dimension 0, may hold values from -6 to 6
- modulation: float32 [6, 4096], P('groups'), parts along dimension 0, may hold values from -3 to 3
- expert_in: bfloat16 [4096, 8192], P(None, 'tile'), may hold values from -0.09375 to 0.09375
- expert_out: bfloat16 [8192, 4096], P('tile'), may hold values from -0.125 to 0.125
- routes: int32 [2048, 2], P(('groups', 'tile')), parts along dimension 0, may hold values from 0 to 3, all different within a row; in each aligned block of 64 rows (0 to 63, 64 to 127, ...) at most 48 rows name the same one
- gate_fixed: int32 [2048, 2], P(('groups', 'tile')), parts along dimension 0, may hold values from 64 to 1023
Outputs:
- layer_out: bfloat16 [2048, 4096], P(('groups', 'tile')), parts along dimension 0
The draws below stay inside these ranges and needn't reach their ends.
There are 2 independent parts, one for each index of `groups`. The reference program is written for one: setup_inputs(seed, part) draws one part's arguments, and reference() takes and returns one part's arrays. A program takes and returns all parts, laid end to end along the dimension named above; an argument that names none is the same for every part. Nothing has to cross between parts.
Inputs may be any that keep to these rules, and one draw needn't show every extreme that they name: `routes`: the two experts of a token differ; among the 64 tokens of one tile no expert is named more than 48 times.
All inputs are finite; a program needn't handle non-finite values.
Results may differ from the reference program's by a relative error of at most 0.011.
Values may be sent and summed in bfloat16 or wider, within the bound.
A program may use at most 128 MiB of HBM per device.

```python
import math
import jax
import jax.numpy as jnp
import numpy as np
from jax import lax

HEAD_DIM = 128
D = 4096
SPLIT = 4
EFF_DEV = 512
TILE_COLS = 8
TOK_DEV = 64
TOKENS = 1024
EXPERTS = 4
CAP = 48
N_TILE = 16


def draw_queries(key, part):
    field = jnp.clip(jax.random.normal(jax.random.fold_in(key, 11), (TOKENS, D), jnp.float32), -4.0, 4.0)
    return field.astype(jnp.bfloat16)


def draw_key_rows(key, part):
    field = jnp.clip(jax.random.normal(jax.random.fold_in(key, 13), (TOKENS, D), jnp.float32), -4.0, 4.0)
    return field.astype(jnp.bfloat16)


def place_ends(values, stream_key, smallest, largest):
    longest = values.shape.index(max(values.shape))
    spots = []
    for shift in (0, 1):
        where = [jax.random.randint(jax.random.fold_in(stream_key, axis), (), 0, length) for axis, length in enumerate(values.shape)]
        where[longest] = (where[longest] + shift) % values.shape[longest]
        spots.append(tuple(where))
    return values.at[spots[0]].set(smallest).at[spots[1]].set(largest)


def block_scale(stream_key, extent, cuts, smallest, high):
    def one(position, parts):
        steps = jax.random.uniform(jax.random.fold_in(jax.random.fold_in(stream_key, 6), position), (parts,), jnp.float32, smallest / len(cuts), high / len(cuts))
        return jnp.repeat(jnp.exp(steps), extent[position] // parts).reshape((-1,) + (1,) * (len(extent) - position - 1))

    loudness = one(*cuts[0])
    for cut in cuts[1:]:
        loudness = loudness * one(*cut)
    return loudness


def routed_block(key, own, number, rows, amount, top, most, slope):
    order = jax.random.permutation(key, amount)
    crowded, ordinary = portions_of(amount, rows * top, most, slope, True), portions_of(amount, rows * top, most, slope, False)
    places = jnp.arange(amount)

    def named(sizes, offset_by):
        used = int((sizes > 0).sum())
        fixed = max(1, used // 4)
        moved = fixed + (places - fixed + offset_by * (used - fixed)) % max(1, amount - fixed)
        return jnp.zeros((amount,), jnp.int32).at[order[jnp.where(places < fixed, places, moved)]].set(jnp.asarray(sizes, jnp.int32))

    sizes = jnp.where(number % 4 == 0, named(crowded, number // 4), named(ordinary, number - number // 4 - 1))
    mixed = jax.random.permutation(jax.random.fold_in(own, 3), amount)
    giver, receiver = mixed[0:amount // 2 * 2:2], mixed[1:amount // 2 * 2:2]
    room = jnp.minimum(sizes[giver] - 1, most - sizes[receiver]) // 2
    room = jnp.where((giver == order[0]) | (receiver == order[0]) | (sizes[receiver] == 0), 0, jnp.maximum(room, 0))
    moved = jax.random.randint(jax.random.fold_in(own, 4), (amount // 2,), 0, 1 << 20) % (room + 1)
    sizes = sizes.at[giver].add(-moved).at[receiver].add(moved)
    members = jnp.searchsorted(jnp.cumsum(sizes), jnp.arange(rows * top), side="right").astype(jnp.int32)
    table = members.reshape(top, rows).T
    table = table[jax.random.permutation(jax.random.fold_in(own, 1), rows)]
    offset_by = jax.random.randint(jax.random.fold_in(own, 2), (rows, 1), 0, top)
    return jnp.take_along_axis(table, (jnp.arange(top)[None, :] + offset_by) % top, axis=1)


def portions_of(amount, total, most, skew, full):
    portions = [(1 << 20) // math.isqrt(grade ** skew) + 1 for grade in range(1, amount + 1)]
    largest = most if full else min(most, max(-(-total // amount), total * portions[0] // sum(portions)))
    least = 1 if total - largest >= amount - 1 else 0
    given, rest = [largest] + [least] * (amount - 1), total - largest - least * (amount - 1)
    while rest > 0:
        candidates = [i for i in range(1, amount) if given[i] < largest] or [i for i in range(1, amount) if given[i] < most]
        mass, budget = sum([portions[i] for i in candidates]), rest
        for i in candidates:
            addition = min(most - given[i], max(1, budget * portions[i] // mass), rest)
            given[i] = given[i] + addition
            rest = rest - addition
    return np.array(given)


def gaussian(key, shape, scale, most, cuts=(), kind=jnp.bfloat16):
    entries = jax.random.normal(key, shape, jnp.float32) * scale
    if len(cuts) > 0:
        entries = block_scale(key, shape, cuts, -0.22, 0.18) * entries
    return jnp.clip(entries, min=-most, max=most).astype(kind)


def setup_inputs(seed: int = 0, part: int = 0) -> dict:
    seeds = jax.random.split(jax.random.key(seed), 9)
    own_keys = jax.random.split(jax.random.fold_in(seeds[8], part), 9)
    queries = draw_queries(jax.random.fold_in(jax.random.fold_in(seeds[8], part), 71), part)
    key_rows = draw_key_rows(jax.random.fold_in(jax.random.fold_in(seeds[8], part), 71), part)
    values = gaussian(own_keys[2], (TOKENS, D), 1.0, 6.0, ((0, 16),))
    modulation = gaussian(own_keys[3], (3, D), 0.5, 3.0, (), jnp.float32)
    expert_in = gaussian(seeds[4], (D, EXPERTS * SPLIT * EFF_DEV), D ** -0.5, 0.09375, ((1, 16),))
    expert_out = gaussian(seeds[5], (EXPERTS * SPLIT * EFF_DEV, D), (SPLIT * EFF_DEV) ** -0.5, 0.125, ((0, 16),))
    routes_keys = jax.random.split(jax.random.fold_in(own_keys[6], 1), TOKENS // TOK_DEV)
    routes_turns = jax.random.permutation(jax.random.fold_in(own_keys[6], 3), TOKENS // TOK_DEV)
    routes = jax.vmap(lambda own, number: routed_block(jax.random.fold_in(own_keys[6], 2), own, number, TOK_DEV, EXPERTS, 2, CAP, 2))(routes_keys, routes_turns).reshape((TOKENS, 2))
    gate_fixed = place_ends(jax.random.randint(own_keys[7], (TOKENS, 2), 64, 1024), jax.random.fold_in(own_keys[7], 1), 64, 1023).astype(jnp.int32)
    return {"queries": queries, "key_rows": key_rows, "values": values, "modulation": modulation, "expert_in": expert_in, "expert_out": expert_out, "routes": routes, "gate_fixed": gate_fixed}


EPSILON = 1e-06
MASKED = -1e+30

def attend_tile(query_block, banded, allowed):
    rows_here = query_block.shape[0]
    heads_count = D // HEAD_DIM
    query_heads = query_block.astype(jnp.float32).reshape(rows_here, heads_count, HEAD_DIM)
    key_heads = banded[0].astype(jnp.float32).reshape(banded.shape[1], heads_count, HEAD_DIM)
    value_heads = banded[1].astype(jnp.float32).reshape(banded.shape[1], heads_count, HEAD_DIM)
    scores = jnp.einsum('qhd,khd->hqk', query_heads, key_heads) * (1.0 / math.sqrt(HEAD_DIM))
    scores = jnp.where(allowed[None, None, :], scores, MASKED)
    highest = lax.optimization_barrier(jnp.max(scores, axis=-1, keepdims=True))
    raised = jnp.exp(scores - highest)
    probs = (raised / lax.optimization_barrier(jnp.sum(raised, axis=-1, keepdims=True))).astype(jnp.bfloat16)
    attended = jnp.einsum('hqk,khd->qhd', probs.astype(jnp.float32), value_heads)
    return attended.reshape(rows_here, D).astype(jnp.bfloat16)

def modulate(attended, modulation):
    wide = attended.astype(jnp.float32)
    center = lax.optimization_barrier(jnp.mean(wide, axis=-1, keepdims=True))
    spread = lax.optimization_barrier(jnp.mean(jnp.square(wide - center), axis=-1, keepdims=True))
    normed = (wide - center) * lax.rsqrt(spread + EPSILON)
    return (normed * (1.0 + modulation[1]) + modulation[0]).astype(jnp.bfloat16)

def slot_table(flat, experts_count):
    onehot = (flat[:, None] == jnp.arange(experts_count, dtype=jnp.int32)[None, :]).astype(jnp.int32)
    before = jnp.cumsum(onehot, axis=0) - onehot
    return lax.optimization_barrier(jnp.sum(before * onehot, axis=1)).astype(jnp.int32)

def expert_apply(rows, first_weight, second_weight):
    hidden = jax.nn.gelu(jnp.dot(rows, first_weight, preferred_element_type=jnp.float32), approximate=True).astype(jnp.bfloat16)
    return jnp.dot(hidden, second_weight, preferred_element_type=jnp.float32).astype(jnp.bfloat16)

def reference(queries, key_rows, values, modulation, expert_in, expert_out, routes, gate_fixed):
    experts_count = N_TILE // SPLIT
    capacity = 3 * TOK_DEV // experts_count
    grid_rows = N_TILE // TILE_COLS
    rotation = TILE_COLS // 2
    blocks = jnp.stack([key_rows, values]).reshape(2, N_TILE, TOK_DEV, D)
    tile_order = jnp.roll(blocks, rotation, axis=1)
    stacked = tile_order.reshape(2, grid_rows, TILE_COLS, TOK_DEV, D)
    padded = jnp.pad(stacked, ((0, 0), (1, 1), (1, 1), (0, 0), (0, 0)))

    def one_block(block_number):
        tile_number = ((block_number + rotation) % N_TILE).astype(jnp.int32)
        grid_row = (tile_number // TILE_COLS).astype(jnp.int32)
        grid_col = (tile_number % TILE_COLS).astype(jnp.int32)
        zero = jnp.zeros((), jnp.int32)
        block = lax.dynamic_slice(padded, (zero, grid_row, grid_col, zero, zero), (2, 3, 3, TOK_DEV, D))
        banded = block.reshape(2, 9 * TOK_DEV, D)
        start = (block_number * TOK_DEV).astype(jnp.int32)
        query_block = lax.dynamic_slice_in_dim(queries, start, TOK_DEV, 0)
        rows_ok = jnp.stack([grid_row > 0, grid_row >= 0, grid_row < grid_rows - 1])
        cols_ok = jnp.stack([grid_col > 0, grid_col >= 0, grid_col < TILE_COLS - 1])
        usable = rows_ok[:, None] & cols_ok[None, :]
        allowed = jnp.broadcast_to(usable[:, :, None], (3, 3, TOK_DEV)).reshape(9 * TOK_DEV)
        return attend_tile(query_block, banded, allowed)
    attended = lax.map(one_block, jnp.arange(N_TILE, dtype=jnp.int32)).reshape(TOKENS, D)
    normed = modulate(attended, modulation)
    tile_routes = routes.reshape(N_TILE, 2 * TOK_DEV)
    slots = jax.vmap(slot_table, in_axes=(0, None))(tile_routes, experts_count)
    sources = jnp.arange(N_TILE, dtype=jnp.int32)[:, None]
    place = (tile_routes * (N_TILE * capacity) + sources * capacity + slots).reshape(-1).astype(jnp.int32)
    token_of = (jnp.arange(2 * TOKENS, dtype=jnp.int32) // 2).astype(jnp.int32)
    table = jnp.full((experts_count * N_TILE * capacity,), TOKENS, jnp.int32).at[place].set(token_of)
    extended = jnp.concatenate([normed, jnp.zeros((1, D), normed.dtype)], axis=0)

    def one_expert(expert):
        chosen = lax.dynamic_slice_in_dim(table, (expert * (N_TILE * capacity)).astype(jnp.int32), N_TILE * capacity, 0)
        rows = jnp.take(extended, chosen, axis=0)
        total = jnp.zeros((N_TILE * capacity, D), jnp.float32)
        for quarter in range(SPLIT):
            column = ((expert * SPLIT + quarter) * EFF_DEV).astype(jnp.int32)
            first_weight = lax.dynamic_slice_in_dim(expert_in, column, EFF_DEV, 1)
            second_weight = lax.dynamic_slice_in_dim(expert_out, column, EFF_DEV, 0)
            total = total + expert_apply(rows, first_weight, second_weight).astype(jnp.float32)
        return total.astype(jnp.bfloat16)
    expert_rows = lax.map(one_expert, jnp.arange(experts_count, dtype=jnp.int32)).reshape(experts_count * N_TILE * capacity, D)
    picked = jnp.take(expert_rows, place, axis=0).reshape(TOKENS, 2, D)
    gate_scale = gate_fixed.astype(jnp.float32) / 1024.0
    mixture = lax.optimization_barrier(jnp.sum(picked.astype(jnp.float32) * gate_scale[:, :, None], axis=1))
    return (attended.astype(jnp.float32) + modulation[2] * mixture).astype(jnp.bfloat16)
```

```python
import functools
import math

import jax
import jax.numpy as jnp
from jax import lax
from jax.experimental import pallas as pl
from jax.experimental.pallas import tpu as pltpu
from jax.sharding import PartitionSpec as P

HEAD_DIM = 128
D = 4096
SPLIT = 4
TILE_COLS = 8
LANES = 128
SUBLANES = 8

EPSILON = 1e-06
MASKED = -1e30
MESH = pl.DeviceIdType.MESH
VMEM_LIMIT = 60 * 1024 * 1024


def when(cond, body):
    if cond is True:
        body()
    else:
        pl.when(cond)(body)


def both(a, b):
    if a is True:
        return b
    if b is True:
        return a
    return jnp.logical_and(a, b)


def remote(src, dst, send_sem, recv_sem, target):
    return pltpu.make_async_remote_copy(
        src_ref=src,
        dst_ref=dst,
        send_sem=send_sem,
        recv_sem=recv_sem,
        device_id={"tile": target},
        device_id_type=MESH,
    )


def halo_levels(n):
    grid_rows = n // TILE_COLS
    if grid_rows < 2:
        return 1
    return 2 if grid_rows == 2 else 3


def attention_kernel(
    n, rows, q_ref, k_ref, v_ref, mod_ref, att_ref, norm_ref, keys, vals, send_sem, recv_sem, own_sem
):
    me = lax.axis_index("tile")
    grid_rows = n // TILE_COLS
    tile = lax.rem(me + TILE_COLS // 2, n)
    row = lax.div(tile, TILE_COLS)
    col = lax.rem(tile, TILE_COLS)
    if grid_rows < 2:
        verticals = []
    elif grid_rows == 2:
        verticals = [(1, TILE_COLS, True, 1)]
    else:
        verticals = [(1, n - TILE_COLS, row > 0, 2), (2, TILE_COLS, row < grid_rows - 1, 1)]
    sides = [(-1, col > 0), (1, col < TILE_COLS - 1)]
    here = {level: exists for level, _, exists, _ in verticals}
    here[0] = True

    def slot(level, side):
        return level * 3 + 1 + side

    def place(buf, s):
        return buf.at[pl.ds(s * rows, rows), :]

    def over(offset):
        return lax.rem(me + offset + n, n)

    own = [
        pltpu.make_async_copy(src, place(buf, slot(0, 0)), own_sem.at[i])
        for i, (src, buf) in enumerate(((k_ref, keys), (v_ref, vals)))
    ]
    for copy in own:
        copy.start()

    barrier = pltpu.get_barrier_semaphore()
    partners = [(over(offset), exists) for _, offset, exists, _ in verticals]
    partners += [(over(side), exists) for side, exists in sides]
    for target, exists in partners:

        def greet(target=target):
            pl.semaphore_signal(barrier, inc=1, device_id={"tile": target}, device_id_type=MESH)

        when(exists, greet)
    expected = sum(1 if exists is True else jnp.where(exists, 1, 0) for _, exists in partners)
    pl.semaphore_wait(barrier, expected)

    sends = []

    def push(srcs, there, target, exists):
        index = len(sends)
        copies = [
            remote(src, place(buf, there), send_sem.at[index, i], recv_sem.at[there, i], target)
            for i, (src, buf) in enumerate(zip(srcs, (keys, vals)))
        ]

        def go():
            for copy in copies:
                copy.start()

        when(exists, go)
        sends.append((copies, exists))

    def arrived(s, exists):
        def go():
            for i, buf in enumerate((keys, vals)):
                remote(place(buf, s), place(buf, s), send_sem.at[0, i], recv_sem.at[s, i], me).wait_recv()

        when(exists, go)

    for level, offset, exists, there in verticals:
        push((k_ref, v_ref), slot(there, 0), over(offset), exists)
    for side, exists in sides:
        push((k_ref, v_ref), slot(0, -side), over(side), exists)
    for s in range(3 * (1 + len(verticals))):
        level, side = s // 3, s % 3 - 1
        exists = here[level]
        for other, side_exists in sides:
            if other == side:
                exists = both(exists, side_exists)
        if exists is True:
            continue

        def clear(s=s):
            for buf in (keys, vals):
                buf[pl.ds(s * rows, rows), :] = jnp.zeros((rows, D), buf.dtype)

        pl.when(jnp.logical_not(exists))(clear)
    for level, offset, exists, there in verticals:
        arrived(slot(level, 0), exists)
        for side, side_exists in sides:
            push(
                (place(keys, slot(level, 0)), place(vals, slot(level, 0))),
                slot(level, -side),
                over(side),
                both(exists, side_exists),
            )
    for copy in own:
        copy.wait()
    for side, side_exists in sides:
        arrived(slot(0, side), side_exists)
    for level, _, exists, _ in verticals:
        for side, side_exists in sides:
            arrived(slot(level, side), both(exists, side_exists))

    span = 3 * (1 + len(verticals)) * rows
    where = lax.broadcasted_iota(jnp.int32, (rows, span), 1)
    bias = jnp.zeros((rows, span), jnp.float32)
    for s in range(span // rows):
        level, side = s // 3, s % 3 - 1
        exists = here[level]
        for other, side_exists in sides:
            if other == side:
                exists = both(exists, side_exists)
        if exists is True:
            continue
        penalty = jnp.where(exists, 0.0, MASKED)
        bias = jnp.where((where >= s * rows) & (where < (s + 1) * rows), penalty, bias)
    scale = 1.0 / math.sqrt(HEAD_DIM)
    together = 4

    def heads(step, carry):
        for extra in range(together):
            at = pl.ds(pl.multiple_of((step * together + extra) * HEAD_DIM, HEAD_DIM), HEAD_DIM)
            scores = lax.dot_general(
                q_ref[:, at], keys[:, at], (((1,), (1,)), ((), ())), preferred_element_type=jnp.float32
            )
            scores = scores * scale + bias
            raised = jnp.exp(scores - jnp.max(scores, axis=-1, keepdims=True))
            probs = (raised * (1.0 / jnp.sum(raised, axis=-1, keepdims=True))).astype(jnp.bfloat16)
            att_ref[:, at] = jnp.dot(probs, vals[:, at], preferred_element_type=jnp.float32).astype(
                att_ref.dtype
            )
        return carry

    lax.fori_loop(0, D // HEAD_DIM // together, heads, 0)

    def normalise(step, carry):
        at = pl.ds(pl.multiple_of(step * 16, 16), 16)
        wide = att_ref[at, :].astype(jnp.float32)
        wide = wide - jnp.mean(wide, axis=-1, keepdims=True)
        spread = jnp.mean(wide * wide, axis=-1, keepdims=True)
        normed = wide * lax.rsqrt(spread + EPSILON)
        norm_ref[at, :] = (normed * (1.0 + mod_ref[1:2, :]) + mod_ref[0:1, :]).astype(norm_ref.dtype)
        return carry

    lax.fori_loop(0, rows // 16, normalise, 0)
    for copies, exists in sends:

        def drain(copies=copies):
            for copy in copies:
                copy.wait_send()

        when(exists, drain)


def attention(queries, key_rows, values, modulation):
    n = lax.axis_size("tile")
    rows = queries.shape[0]
    levels = halo_levels(n)
    slots = 3 * levels
    vmem = pl.BlockSpec(memory_space=pltpu.VMEM)
    hbm = pl.BlockSpec(memory_space=pl.ANY)
    return pl.pallas_call(
        functools.partial(attention_kernel, n, rows),
        name="halo_attention",
        out_shape=(
            jax.ShapeDtypeStruct((rows, D), jnp.bfloat16),
            jax.ShapeDtypeStruct((rows, D), jnp.bfloat16),
        ),
        in_specs=[vmem, hbm, hbm, vmem],
        out_specs=(vmem, vmem),
        scratch_shapes=[
            pltpu.VMEM((slots * rows, D), jnp.bfloat16),
            pltpu.VMEM((slots * rows, D), jnp.bfloat16),
            pltpu.SemaphoreType.DMA((2 + 3 * (levels - 1), 2)),
            pltpu.SemaphoreType.DMA((slots, 2)),
            pltpu.SemaphoreType.DMA((2,)),
        ],
        compiler_params=pltpu.CompilerParams(
            collective_id=0, has_side_effects=True, vmem_limit_bytes=VMEM_LIMIT
        ),
    )(queries, key_rows, values, modulation)


def plane_order(planes):
    order = [0]
    for step in range(1, planes // 2 + 1):
        for d in (step, planes - step):
            if d not in order:
                order.append(d)
    return order


def expert_kernel(
    n, rows, norm_ref, att_ref, mod_ref, gate_ref, first_ref, second_ref, out_ref,
    tokens, gates, first, second, hidden, part, r1, r2, r3a, r3b, r4,
    send_sem, token_sem, gate_sem, s1_sem, s2_sem, s3a_sem, s3b_sem, s4_sem, own_sem,
):
    planes = n // SPLIT
    half = rows // 2
    width = first_ref.shape[1]
    me = lax.axis_index("tile")
    p = lax.div(me, SPLIT)
    q = lax.rem(me, SPLIT)
    y = lax.div(q, 2)
    c = lax.rem(q, 2)
    order = plane_order(planes)

    def device(plane, yy, cc):
        return plane * SPLIT + yy * 2 + cc

    beside = device(p, 1 - y, c)
    twin = device(p, y, 1 - c)
    plane_of = {d: lax.rem(p + d, planes) for d in order}

    loads = [
        pltpu.make_async_copy(norm_ref, tokens.at[pl.ds(pl.multiple_of(me * rows, rows), rows), :], own_sem.at[0]),
        pltpu.make_async_copy(gate_ref, gates.at[me], own_sem.at[1]),
        pltpu.make_async_copy(first_ref, first, own_sem.at[2]),
        pltpu.make_async_copy(second_ref, second, own_sem.at[3]),
    ]
    for load in loads:
        load.start()

    barrier = pltpu.get_barrier_semaphore()
    for step in range(1, n):
        pl.semaphore_signal(
            barrier, inc=1, device_id={"tile": lax.rem(me + step, n)}, device_id_type=MESH
        )
    pl.semaphore_wait(barrier, n - 1)

    sends = []

    def push(src, dst, recv, target):
        copy = remote(src, dst, send_sem.at[len(sends)], recv, target)
        copy.start()
        sends.append(copy)

    def landed(dst, recv):
        remote(dst, dst, send_sem.at[0], recv, me).wait_recv()

    def block(buf, index, size, offset=0, count=None):
        return buf.at[pl.ds(pl.multiple_of(index * size + offset, half), count or size), :]

    def piece(tile, h):
        return block(tokens, tile, rows, h * half, half)

    def give(tile, h, target):
        push(piece(tile, h), piece(tile, h), token_sem.at[tile, h], target)

    def take(tile, h):
        landed(piece(tile, h), token_sem.at[tile, h])

    loads[0].wait()
    loads[1].wait()
    give(me, 0, beside)
    for d in order[1:]:
        give(me, 1, device(plane_of[d], y, c))
    for h in (0, 1):
        give(me, h, twin)
    give(me, 1, beside)
    for d in order[1:]:
        give(me, 0, device(plane_of[d], y, c))
    for step in range(1, n):
        push(gates.at[me], gates.at[me], gate_sem.at[me], lax.rem(me + step, n))
    take(beside, 0)
    for d in order[1:]:
        give(beside, 0, device(plane_of[d], y, c))
    give(beside, 0, twin)
    take(beside, 1)
    give(beside, 1, twin)

    def forward(d):
        tile = device(plane_of[d], y, c)
        take(tile, 1)
        give(tile, 1, beside)
        give(tile, 1, twin)
        take(tile, 0)
        give(tile, 0, twin)

    def forward_more(d):
        tile = device(plane_of[d], 1 - y, c)
        for h in (0, 1):
            take(tile, h)
            give(tile, h, twin)

    group = SPLIT * rows
    chunk = min(width, 256)
    chunk_out = 512
    eye = lax.broadcasted_iota(jnp.int32, (rows, LANES), 0) == lax.broadcasted_iota(
        jnp.int32, (rows, LANES), 1
    )

    def compute(d):
        plane = plane_of[d]
        for yy in (0, 1):
            for h in (0, 1):
                take(device(plane, yy, 1 - c), h)
        for k in range(SPLIT):
            tile = plane * SPLIT + k
            if d == 0:

                @pl.when(tile != me)
                def _(tile=tile):
                    landed(gates.at[tile], gate_sem.at[tile])
            else:
                landed(gates.at[tile], gate_sem.at[tile])
        at = pl.ds(pl.multiple_of(plane * group, group), group)
        columns = []
        for k in range(SPLIT):
            line = gates[plane * SPLIT + k, pl.ds(p, 1), :]
            columns.append(jnp.sum(jnp.where(eye, line, 0.0), axis=1, keepdims=True))
        weight = jnp.concatenate(columns, axis=0)

        def one(step, carry):
            cols = pl.ds(pl.multiple_of(step * chunk, chunk), chunk)
            raw = jnp.dot(tokens[at, :], first[:, cols], preferred_element_type=jnp.float32)
            hidden[:, cols] = jax.nn.gelu(raw, approximate=True).astype(hidden.dtype)
            return carry

        lax.fori_loop(0, width // chunk, one, 0)

        def two(step, carry):
            cols = pl.ds(pl.multiple_of(step * chunk_out, chunk_out), chunk_out)
            raw = jnp.dot(hidden[...], second[:, cols], preferred_element_type=jnp.float32)
            part[at, cols] = (raw * weight).astype(part.dtype)
            return carry

        lax.fori_loop(0, D // chunk_out, two, 0)
        for yy in (0, 1):
            push(
                block(part, device(plane, yy, 1 - c), rows),
                block(r1, plane * 2 + yy, rows),
                s1_sem.at[plane, yy],
                twin,
            )

    def add(dst, start, terms, count):
        def body(step, carry):
            at = pl.ds(pl.multiple_of(start + step * 16, 16), 16)
            total = dst[at, :].astype(jnp.float32)
            for buf, base in terms:
                total = total + buf[pl.ds(pl.multiple_of(base + step * 16, 16), 16), :].astype(jnp.float32)
            dst[at, :] = total.astype(dst.dtype)
            return carry

        lax.fori_loop(0, count // 16, body, 0)

    def fold_twin(d):
        plane = plane_of[d]
        for yy in (0, 1):
            landed(block(r1, plane * 2 + yy, rows), s1_sem.at[plane, yy])
            add(part, device(plane, yy, c) * rows, [(r1, (plane * 2 + yy) * rows)], rows)
            if d != 0:
                push(
                    block(part, device(plane, yy, c), rows, half, half),
                    block(r3b, p * 2 + yy, half),
                    s3b_sem.at[p, yy],
                    device(plane, y, c),
                )
        push(
            block(part, device(plane, 1 - y, c), rows, 0, half),
            block(r2, plane, half),
            s2_sem.at[plane],
            beside,
        )

    def fold_beside(d):
        plane = plane_of[d]
        landed(block(r2, plane, half), s2_sem.at[plane])
        tile = device(plane, y, c)
        add(part, tile * rows, [(r2, plane * half)], half)
        if d != 0:
            push(
                block(part, tile, rows, 0, half),
                block(r3a, p, half),
                s3a_sem.at[p],
                device(plane, y, c),
            )

    for load in loads[2:]:
        load.wait()
    compute(0)
    for d in order[1:]:
        forward(d)
    for i, d in enumerate(order):
        if i >= 1:
            forward_more(d)
            compute(d)
            fold_twin(order[i - 1])
        if i >= 2:
            fold_beside(order[i - 2])
    fold_twin(order[-1])
    for d in order[-2:]:
        fold_beside(d)

    others = [plane_of[d] for d in order[1:]]
    for source in others:
        landed(block(r3b, source * 2 + 1 - y, half), s3b_sem.at[source, 1 - y])
    add(
        part,
        beside * rows + half,
        [(r3b, (source * 2 + 1 - y) * half) for source in others],
        half,
    )
    push(block(part, beside, rows, half, half), r4, s4_sem, beside)
    for source in others:
        landed(block(r3b, source * 2 + y, half), s3b_sem.at[source, y])
    for source in others:
        landed(block(r3a, source, half), s3a_sem.at[source])
    landed(r4, s4_sem)

    def finish(terms, base):
        def body(step, carry):
            total = None
            for buf, start in terms:
                value = buf[pl.ds(pl.multiple_of(start + step * 16, 16), 16), :].astype(jnp.float32)
                total = value if total is None else total + value
            at = pl.ds(pl.multiple_of(base + step * 16, 16), 16)
            out_ref[at, :] = (att_ref[at, :].astype(jnp.float32) + mod_ref[2:3, :] * total).astype(
                out_ref.dtype
            )
            return carry

        lax.fori_loop(0, half // 16, body, 0)

    finish([(part, me * rows)] + [(r3a, source * half) for source in others], 0)
    finish(
        [(part, me * rows + half), (r4, 0)] + [(r3b, (source * 2 + y) * half) for source in others],
        half,
    )
    for copy in sends:
        copy.wait_send()


def dense_bytes(n, rows, width):
    planes = n // SPLIT
    half = rows // 2
    lines = 2 * n * rows + planes * 2 * rows + 4 * planes * half + half + 3 * rows
    return 2 * (lines * D + 2 * width * D)


def experts_dense(normed, attended, modulation, expert_in, expert_out, routes, gate_fixed):
    n = lax.axis_size("tile")
    rows = normed.shape[0]
    width = expert_in.shape[1]
    planes = n // SPLIT
    half = rows // 2
    lines = -(-planes // SUBLANES) * SUBLANES
    named = routes[None, :, :] == jnp.arange(lines, dtype=jnp.int32)[:, None, None]
    gates = jnp.sum(jnp.where(named, gate_fixed.astype(jnp.float32)[None] / 1024.0, 0.0), axis=2)
    gates = jnp.pad(gates, ((0, 0), (0, LANES - rows)))
    vmem = pl.BlockSpec(memory_space=pltpu.VMEM)
    hbm = pl.BlockSpec(memory_space=pl.ANY)
    dma = pltpu.SemaphoreType.DMA
    count_sends = 5 + 2 * (planes - 1) + (n - 1) + (planes - 1) + 1 + 7 * planes + 2 * planes + 8
    bf = jnp.bfloat16
    return pl.pallas_call(
        functools.partial(expert_kernel, n, rows),
        name="dense_experts",
        out_shape=jax.ShapeDtypeStruct((rows, D), bf),
        in_specs=[hbm, vmem, vmem, hbm, hbm, hbm],
        out_specs=vmem,
        scratch_shapes=[
            pltpu.VMEM((n * rows, D), bf),
            pltpu.VMEM((n, lines, LANES), jnp.float32),
            pltpu.VMEM((D, width), bf),
            pltpu.VMEM((width, D), bf),
            pltpu.VMEM((SPLIT * rows, width), bf),
            pltpu.VMEM((n * rows, D), bf),
            pltpu.VMEM((planes * 2 * rows, D), bf),
            pltpu.VMEM((planes * half, D), bf),
            pltpu.VMEM((planes * half, D), bf),
            pltpu.VMEM((planes * 2 * half, D), bf),
            pltpu.VMEM((half, D), bf),
            dma((count_sends * 2,)),
            dma((n, 2)),
            dma((n,)),
            dma((planes, 2)),
            dma((planes,)),
            dma((planes,)),
            dma((planes, 2)),
            dma(()),
            dma((4,)),
        ],
        compiler_params=pltpu.CompilerParams(
            collective_id=1, has_side_effects=True, vmem_limit_bytes=VMEM_LIMIT
        ),
    )(normed, attended, modulation, gates, expert_in, expert_out)


def slot_table(flat, experts_count):
    onehot = (flat[:, None] == jnp.arange(experts_count, dtype=jnp.int32)[None, :]).astype(
        jnp.int32
    )
    before = jnp.cumsum(onehot, axis=0) - onehot
    return jnp.sum(before * onehot, axis=1)


def expert_apply(rows, first_weight, second_weight):
    hidden = jax.nn.gelu(
        jnp.dot(rows, first_weight, preferred_element_type=jnp.float32), approximate=True
    ).astype(jnp.bfloat16)
    return jnp.dot(hidden, second_weight, preferred_element_type=jnp.float32).astype(jnp.bfloat16)


def experts_sparse(normed, attended, modulation, expert_in, expert_out, routes, gate_fixed):
    devices = lax.axis_size("tile")
    rows_dev = normed.shape[0]
    experts_count = devices // SPLIT
    capacity = 3 * rows_dev // experts_count
    flat = routes.reshape(-1)
    slots = slot_table(flat, experts_count)
    target = flat * capacity + slots
    chooser = (
        target[None, :] == jnp.arange(experts_count * capacity, dtype=jnp.int32)[:, None]
    ).astype(jnp.bfloat16)
    chooser = chooser.reshape(experts_count * capacity, rows_dev, 2).sum(axis=2)
    buffer = jnp.dot(chooser, normed, preferred_element_type=jnp.float32).astype(jnp.bfloat16)
    copies = jnp.broadcast_to(
        buffer.reshape(experts_count, 1, capacity, D), (experts_count, SPLIT, capacity, D)
    ).reshape(devices, capacity, D)
    received = lax.all_to_all(copies, "tile", split_axis=0, concat_axis=0, tiled=True)
    sources = received.shape[0]
    count = received.shape[1]
    partial_value = expert_apply(received.reshape(sources * count, D), expert_in, expert_out)
    returned = lax.all_to_all(
        partial_value.reshape(sources, count, D), "tile", split_axis=0, concat_axis=0, tiled=True
    )
    summed = jnp.sum(
        returned.reshape(experts_count, SPLIT, capacity, D).astype(jnp.float32), axis=1
    )
    expert_rows = summed.astype(jnp.bfloat16).reshape(experts_count * capacity, D)
    picked = jnp.take(expert_rows, target, axis=0).reshape(rows_dev, 2, D)
    gate_scale = gate_fixed.astype(jnp.float32) / 1024.0
    mixture = jnp.sum(picked.astype(jnp.float32) * gate_scale[:, :, None], axis=1)
    return (attended.astype(jnp.float32) + modulation[2] * mixture).astype(jnp.bfloat16)


def shards(queries, key_rows, values, modulation, expert_in, expert_out, routes, gate_fixed):
    attended, normed = attention(queries, key_rows, values, modulation)
    n = lax.axis_size("tile")
    fits = dense_bytes(n, queries.shape[0], expert_in.shape[1]) < VMEM_LIMIT * 3 // 4
    experts = experts_dense if fits else experts_sparse
    return experts(normed, attended, modulation, expert_in, expert_out, routes, gate_fixed)


def solution(mesh):
    placed = (
        P(("groups", "tile"), None),
        P(("groups", "tile"), None),
        P(("groups", "tile"), None),
        P("groups", None),
        P(None, "tile"),
        P("tile", None),
        P(("groups", "tile"), None),
        P(("groups", "tile"), None),
    )
    return jax.shard_map(
        shards, mesh=mesh, in_specs=placed, out_specs=P(("groups", "tile"), None), check_vma=False
    )
```

```python
import functools
import math

import jax
import jax.numpy as jnp
from jax import lax
from jax.experimental import pallas as pl
from jax.experimental.pallas import tpu as pltpu
from jax.sharding import PartitionSpec as P

HEAD_DIM = 128
D = 4096
SPLIT = 4
TILE_COLS = 8

EPSILON = 1e-06
MASKED = -1e30
MESH = pl.DeviceIdType.MESH
VMEM_LIMIT = 60 * 1024 * 1024


def when(cond, body):
    if cond is True:
        body()
    else:
        pl.when(cond)(body)


def both(a, b):
    if a is True:
        return b
    if b is True:
        return a
    return jnp.logical_and(a, b)


def remote(src, dst, send_sem, recv_sem, target):
    return pltpu.make_async_remote_copy(
        src_ref=src,
        dst_ref=dst,
        send_sem=send_sem,
        recv_sem=recv_sem,
        device_id={"tile": target},
        device_id_type=MESH,
    )


def halo_levels(n):
    grid_rows = n // TILE_COLS
    if grid_rows < 2:
        return 1
    return 2 if grid_rows == 2 else 3


def attention_kernel(
    n, rows, q_ref, k_ref, v_ref, mod_ref, att_ref, norm_ref, keys, vals, send_sem, recv_sem, own_sem
):
    me = lax.axis_index("tile")
    grid_rows = n // TILE_COLS
    tile = lax.rem(me + TILE_COLS // 2, n)
    row = lax.div(tile, TILE_COLS)
    col = lax.rem(tile, TILE_COLS)
    if grid_rows < 2:
        verticals = []
    elif grid_rows == 2:
        verticals = [(1, TILE_COLS, True, 1)]
    else:
        verticals = [(1, n - TILE_COLS, row > 0, 2), (2, TILE_COLS, row < grid_rows - 1, 1)]
    sides = [(-1, col > 0), (1, col < TILE_COLS - 1)]
    here = {level: exists for level, _, exists, _ in verticals}
    here[0] = True

    def slot(level, side):
        return level * 3 + 1 + side

    def place(buf, s):
        return buf.at[pl.ds(s * rows, rows), :]

    def over(offset):
        return lax.rem(me + offset + n, n)

    half = rows // 2
    middle = TILE_COLS // 2
    crossing = {side: col == (middle if side < 0 else middle - 1) for side, _ in sides}
    two = grid_rows == 2

    def part_of(buf, s, h):
        return buf.at[pl.ds(pl.multiple_of(s * rows + h * half, half), half), :]

    own = [
        pltpu.make_async_copy(src, place(buf, slot(0, 0)), own_sem.at[i])
        for i, (src, buf) in enumerate(((k_ref, keys), (v_ref, vals)))
    ]
    for copy in own:
        copy.start()

    def beside(side):
        if not two:
            return over(side)
        return jnp.where(crossing[side], over(side + TILE_COLS), over(side))

    def level_there(level, side):
        return jnp.where(crossing[side], 1 - level, level) if two else level

    barrier = pltpu.get_barrier_semaphore()
    partners = [(over(offset), exists) for _, offset, exists, _ in verticals]
    partners += [(beside(side), exists) for side, exists in sides]
    for target, exists in partners:

        def greet(target=target):
            pl.semaphore_signal(barrier, inc=1, device_id={"tile": target}, device_id_type=MESH)

        when(exists, greet)
    expected = sum(1 if exists is True else jnp.where(exists, 1, 0) for _, exists in partners)
    pl.semaphore_wait(barrier, expected)

    sends = []
    pieces = [(i, h) for i in (0, 1) for h in (0, 1)]
    bufs = (keys, vals)

    def push(i, h, src, there, target, exists):
        copy = remote(
            src,
            part_of(bufs[i], there, h),
            send_sem.at[len(sends)],
            recv_sem.at[there, i * 2 + h],
            target,
        )
        when(exists, copy.start)
        sends.append((copy, exists))

    def arrived(s, exists, i, h):
        ref = part_of(bufs[i], s, h)
        when(exists, remote(ref, ref, send_sem.at[0], recv_sem.at[s, i * 2 + h], me).wait_recv)

    def own_part(i, h):
        return (k_ref, v_ref)[i].at[pl.ds(h * half, half), :]

    for i, h in pieces:
        for level, offset, exists, there in verticals:
            push(i, h, own_part(i, h), slot(there, 0), over(offset), exists)
    for i, h in pieces:
        for side, exists in sides:
            push(i, h, own_part(i, h), slot(level_there(0, side), -side), beside(side), exists)
    for s in range(3 * (1 + len(verticals))):
        level, side = s // 3, s % 3 - 1
        exists = here[level]
        for other, side_exists in sides:
            if other == side:
                exists = both(exists, side_exists)
        if exists is True:
            continue

        def clear(s=s):
            for buf in (keys, vals):
                buf[pl.ds(s * rows, rows), :] = jnp.zeros((rows, D), buf.dtype)

        pl.when(jnp.logical_not(exists))(clear)
    for i, h in pieces:
        for level, offset, exists, there in verticals:
            arrived(slot(level, 0), exists, i, h)
            for side, side_exists in sides:
                push(
                    i,
                    h,
                    part_of(bufs[i], slot(level, 0), h),
                    slot(level_there(level, side), -side),
                    beside(side),
                    both(exists, side_exists),
                )
    for copy in own:
        copy.wait()
    for i, h in pieces:
        for level, exists in sorted(here.items(), key=lambda item: item[0]):
            for side, side_exists in sides:
                arrived(slot(level, side), both(exists, side_exists), i, h)

    span = 3 * (1 + len(verticals)) * rows
    where = lax.broadcasted_iota(jnp.int32, (rows, span), 1)
    bias = jnp.zeros((rows, span), jnp.float32)
    for s in range(span // rows):
        level, side = s // 3, s % 3 - 1
        exists = here[level]
        for other, side_exists in sides:
            if other == side:
                exists = both(exists, side_exists)
        if exists is True:
            continue
        penalty = jnp.where(exists, 0.0, MASKED)
        bias = jnp.where((where >= s * rows) & (where < (s + 1) * rows), penalty, bias)
    scale = 1.0 / math.sqrt(HEAD_DIM)
    together = 4

    def heads(step, carry):
        for extra in range(together):
            at = pl.ds(pl.multiple_of((step * together + extra) * HEAD_DIM, HEAD_DIM), HEAD_DIM)
            scores = lax.dot_general(
                q_ref[:, at], keys[:, at], (((1,), (1,)), ((), ())), preferred_element_type=jnp.float32
            )
            scores = scores * scale + bias
            raised = jnp.exp(scores - jnp.max(scores, axis=-1, keepdims=True))
            probs = (raised * (1.0 / jnp.sum(raised, axis=-1, keepdims=True))).astype(jnp.bfloat16)
            att_ref[:, at] = jnp.dot(probs, vals[:, at], preferred_element_type=jnp.float32).astype(
                att_ref.dtype
            )
        return carry

    lax.fori_loop(0, D // HEAD_DIM // together, heads, 0)

    def normalise(step, carry):
        at = pl.ds(pl.multiple_of(step * 16, 16), 16)
        wide = att_ref[at, :].astype(jnp.float32)
        wide = wide - jnp.mean(wide, axis=-1, keepdims=True)
        spread = jnp.mean(wide * wide, axis=-1, keepdims=True)
        normed = wide * lax.rsqrt(spread + EPSILON)
        norm_ref[at, :] = (normed * (1.0 + mod_ref[1:2, :]) + mod_ref[0:1, :]).astype(norm_ref.dtype)
        return carry

    lax.fori_loop(0, rows // 16, normalise, 0)
    for copy, exists in sends:
        when(exists, copy.wait_send)


def attention(queries, key_rows, values, modulation):
    n = lax.axis_size("tile")
    rows = queries.shape[0]
    levels = halo_levels(n)
    slots = 3 * levels
    vmem = pl.BlockSpec(memory_space=pltpu.VMEM)
    hbm = pl.BlockSpec(memory_space=pl.ANY)
    return pl.pallas_call(
        functools.partial(attention_kernel, n, rows),
        name="halo_attention",
        out_shape=(
            jax.ShapeDtypeStruct((rows, D), jnp.bfloat16),
            jax.ShapeDtypeStruct((rows, D), jnp.bfloat16),
        ),
        in_specs=[vmem, hbm, hbm, vmem],
        out_specs=(vmem, vmem),
        scratch_shapes=[
            pltpu.VMEM((slots * rows, D), jnp.bfloat16),
            pltpu.VMEM((slots * rows, D), jnp.bfloat16),
            pltpu.SemaphoreType.DMA((4 * (2 + 3 * (levels - 1)),)),
            pltpu.SemaphoreType.DMA((slots, 4)),
            pltpu.SemaphoreType.DMA((2,)),
        ],
        compiler_params=pltpu.CompilerParams(
            collective_id=0, has_side_effects=True, vmem_limit_bytes=VMEM_LIMIT
        ),
    )(queries, key_rows, values, modulation)


def nearest_first(p, planes):
    order = [p] + [p * 0] * (planes - 1)
    count = p * 0 + 1
    for step in range(1, planes):
        for other in (p - step, p + step):
            exists = jnp.logical_and(other >= 0, other < planes)
            for i in range(1, planes):
                order[i] = jnp.where(jnp.logical_and(exists, count == i), other, order[i])
            count = count + jnp.where(exists, 1, 0)
    return order


def expert_kernel(
    n, rows, cap, slots_ref, att_ref, mod_ref, high_ref, low_ref, first_ref, second_ref, out_ref,
    tokens, first, second, hidden, part, r1, r2, r3,
    send_sem, token_sem, s1_sem, s2_sem, s3_sem, own_sem,
):
    planes = n // SPLIT
    width = first_ref.shape[1]
    me = lax.axis_index("tile")
    p = lax.div(me, SPLIT)
    q = lax.rem(me, SPLIT)
    y = lax.div(q, 2)
    c = lax.rem(q, 2)
    plane_of = nearest_first(p, planes)

    def device(plane, yy, cc):
        return plane * SPLIT + yy * 2 + cc

    beside = device(p, 1 - y, c)
    twin = device(p, y, 1 - c)

    def block(buf, index):
        return buf.at[pl.ds(pl.multiple_of(index * cap, 16), cap), :]

    loads = [
        pltpu.make_async_copy(block(slots_ref, p), block(tokens, me), own_sem.at[0]),
        pltpu.make_async_copy(first_ref, first, own_sem.at[1]),
        pltpu.make_async_copy(second_ref, second, own_sem.at[2]),
    ]
    for load in loads:
        load.start()

    barrier = pltpu.get_barrier_semaphore()
    targets = [beside, twin] + [device(plane, y, c) for plane in plane_of[1:]]
    for target in targets:
        pl.semaphore_signal(barrier, inc=1, device_id={"tile": target}, device_id_type=MESH)
    pl.semaphore_wait(barrier, len(targets))

    sends = []

    def push(src, dst, recv, target):
        copy = remote(src, dst, send_sem.at[len(sends)], recv, target)
        copy.start()
        sends.append(copy)

    def landed(dst, recv):
        remote(dst, dst, send_sem.at[0], recv, me).wait_recv()

    def give(tile, target):
        push(block(tokens, tile), block(tokens, tile), token_sem.at[tile], target)

    def take(tile):
        landed(block(tokens, tile), token_sem.at[tile])

    for target in (beside, twin):
        push(block(slots_ref, p), block(tokens, me), token_sem.at[me], target)
    for plane in plane_of[1:]:
        push(block(slots_ref, plane), block(tokens, me), token_sem.at[me], device(plane, y, c))

    def forward(i):
        tile = device(plane_of[i], y, c)
        take(tile)
        give(tile, beside)
        give(tile, twin)

    def forward_more(i):
        tile = device(plane_of[i], 1 - y, c)
        take(tile)
        give(tile, twin)

    group = SPLIT * cap
    chunk = min(width, 256)
    chunk_out = 512

    def compute(i):
        plane = plane_of[i]
        for yy in (0, 1):
            take(device(plane, yy, 1 - c))
        at = pl.ds(pl.multiple_of(plane * group, 16), group)

        def one(step, carry):
            cols = pl.ds(pl.multiple_of(step * chunk, chunk), chunk)
            raw = jnp.dot(tokens[at, :], first[:, cols], preferred_element_type=jnp.float32)
            hidden[:, cols] = jax.nn.gelu(raw, approximate=True).astype(hidden.dtype)
            return carry

        lax.fori_loop(0, width // chunk, one, 0)

        def two(step, carry):
            cols = pl.ds(pl.multiple_of(step * chunk_out, chunk_out), chunk_out)
            raw = jnp.dot(hidden[...], second[:, cols], preferred_element_type=jnp.float32)
            part[at, cols] = raw.astype(part.dtype)
            return carry

        lax.fori_loop(0, D // chunk_out, two, 0)
        for yy in (0, 1):
            push(
                block(part, device(plane, yy, 1 - c)),
                block(r1, plane * 2 + yy),
                s1_sem.at[plane, yy],
                twin,
            )

    def add(tile, other, index):
        def body(step, carry):
            at = pl.ds(pl.multiple_of(tile * cap + step * 16, 16), 16)
            extra = other[pl.ds(pl.multiple_of(index * cap + step * 16, 16), 16), :]
            part[at, :] = (part[at, :].astype(jnp.float32) + extra.astype(jnp.float32)).astype(part.dtype)
            return carry

        lax.fori_loop(0, cap // 16, body, 0)

    def fold_twin(i):
        plane = plane_of[i]
        for yy in (1 - y, y):
            landed(block(r1, plane * 2 + yy), s1_sem.at[plane, yy])
            add(device(plane, yy, c), r1, plane * 2 + yy)
            if yy is not y:
                push(block(part, device(plane, yy, c)), block(r2, plane), s2_sem.at[plane], beside)

    def fold_beside(i):
        plane = plane_of[i]
        landed(block(r2, plane), s2_sem.at[plane])
        tile = device(plane, y, c)
        if i == 0:

            def body(step, carry):
                at = pl.ds(pl.multiple_of(p * cap + step * 16, 16), 16)
                mine = part[pl.ds(pl.multiple_of(me * cap + step * 16, 16), 16), :]
                r3[at, :] = (mine.astype(jnp.float32) + r2[at, :].astype(jnp.float32)).astype(r3.dtype)
                return carry

            lax.fori_loop(0, cap // 16, body, 0)
        else:
            add(tile, r2, plane)
            push(block(part, tile), block(r3, p), s3_sem.at[p], tile)

    loads[0].wait()
    take(beside)
    give(beside, twin)
    for load in loads[1:]:
        load.wait()
    if planes > 1:
        forward(1)
    compute(0)
    for i in range(1, planes):
        if i + 1 < planes:
            forward(i + 1)
        forward_more(i)
        compute(i)
        fold_twin(i - 1)
        if i >= 2:
            fold_beside(i - 2)
    fold_twin(planes - 1)
    for i in range(max(planes - 2, 0), planes):
        fold_beside(i)
    for plane in plane_of[1:]:
        landed(block(r3, plane), s3_sem.at[plane])

    def finish(step, carry):
        cols = pl.ds(pl.multiple_of(step * chunk_out, chunk_out), chunk_out)
        found = r3[:, cols]
        mixture = jnp.dot(high_ref[...], found, preferred_element_type=jnp.float32)
        mixture = mixture + jnp.dot(low_ref[...], found, preferred_element_type=jnp.float32)
        out_ref[:, cols] = (
            att_ref[:, cols].astype(jnp.float32) + mod_ref[2:3, cols] * mixture
        ).astype(out_ref.dtype)
        return carry

    lax.fori_loop(0, D // chunk_out, finish, 0)
    for copy in sends:
        copy.wait_send()


def kernel_bytes(n, cap, width):
    planes = n // SPLIT
    lines = 2 * n * cap + planes * 4 * cap
    return 2 * (lines * D + 2 * width * D)


def experts_kernel(normed, attended, modulation, expert_in, expert_out, routes, gate_fixed):
    n = lax.axis_size("tile")
    rows = normed.shape[0]
    width = expert_in.shape[1]
    planes = n // SPLIT
    cap = 3 * rows // planes
    flat = routes.reshape(-1)
    target = flat * cap + slot_table(flat, planes)
    hit = (target[None, :] == jnp.arange(planes * cap, dtype=jnp.int32)[:, None]).astype(jnp.float32)
    chooser = hit.reshape(planes * cap, rows, 2).sum(axis=2).astype(jnp.bfloat16)
    gates = (hit * (gate_fixed.reshape(-1).astype(jnp.float32) / 1024.0)[None, :]).reshape(
        planes * cap, rows, 2
    ).sum(axis=2).T
    coarse = jnp.floor(gates * 128.0) / 128.0
    high = coarse.astype(jnp.bfloat16)
    low = (gates - coarse).astype(jnp.bfloat16)
    slots = jnp.dot(chooser, normed, preferred_element_type=jnp.float32).astype(jnp.bfloat16)
    vmem = pl.BlockSpec(memory_space=pltpu.VMEM)
    hbm = pl.BlockSpec(memory_space=pl.ANY)
    dma = pltpu.SemaphoreType.DMA
    count_sends = 8 * planes + 8
    bf = jnp.bfloat16
    return pl.pallas_call(
        functools.partial(expert_kernel, n, rows, cap),
        name="routed_experts",
        out_shape=jax.ShapeDtypeStruct((rows, D), bf),
        in_specs=[hbm, vmem, vmem, vmem, vmem, hbm, hbm],
        out_specs=vmem,
        scratch_shapes=[
            pltpu.VMEM((n * cap, D), bf),
            pltpu.VMEM((D, width), bf),
            pltpu.VMEM((width, D), bf),
            pltpu.VMEM((SPLIT * cap, width), bf),
            pltpu.VMEM((n * cap, D), bf),
            pltpu.VMEM((planes * 2 * cap, D), bf),
            pltpu.VMEM((planes * cap, D), bf),
            pltpu.VMEM((planes * cap, D), bf),
            dma((count_sends,)),
            dma((n,)),
            dma((planes, 2)),
            dma((planes,)),
            dma((planes,)),
            dma((3,)),
        ],
        compiler_params=pltpu.CompilerParams(
            collective_id=1, has_side_effects=True, vmem_limit_bytes=VMEM_LIMIT
        ),
    )(slots, attended, modulation, high, low, expert_in, expert_out)


def slot_table(flat, experts_count):
    onehot = (flat[:, None] == jnp.arange(experts_count, dtype=jnp.int32)[None, :]).astype(
        jnp.int32
    )
    before = jnp.cumsum(onehot, axis=0) - onehot
    return jnp.sum(before * onehot, axis=1)


def expert_apply(rows, first_weight, second_weight):
    hidden = jax.nn.gelu(
        jnp.dot(rows, first_weight, preferred_element_type=jnp.float32), approximate=True
    ).astype(jnp.bfloat16)
    return jnp.dot(hidden, second_weight, preferred_element_type=jnp.float32).astype(jnp.bfloat16)


def experts_sparse(normed, attended, modulation, expert_in, expert_out, routes, gate_fixed):
    devices = lax.axis_size("tile")
    rows_dev = normed.shape[0]
    experts_count = devices // SPLIT
    capacity = 3 * rows_dev // experts_count
    flat = routes.reshape(-1)
    slots = slot_table(flat, experts_count)
    target = flat * capacity + slots
    chooser = (
        target[None, :] == jnp.arange(experts_count * capacity, dtype=jnp.int32)[:, None]
    ).astype(jnp.bfloat16)
    chooser = chooser.reshape(experts_count * capacity, rows_dev, 2).sum(axis=2)
    buffer = jnp.dot(chooser, normed, preferred_element_type=jnp.float32).astype(jnp.bfloat16)
    copies = jnp.broadcast_to(
        buffer.reshape(experts_count, 1, capacity, D), (experts_count, SPLIT, capacity, D)
    ).reshape(devices, capacity, D)
    received = lax.all_to_all(copies, "tile", split_axis=0, concat_axis=0, tiled=True)
    sources = received.shape[0]
    count = received.shape[1]
    partial_value = expert_apply(received.reshape(sources * count, D), expert_in, expert_out)
    returned = lax.all_to_all(
        partial_value.reshape(sources, count, D), "tile", split_axis=0, concat_axis=0, tiled=True
    )
    summed = jnp.sum(
        returned.reshape(experts_count, SPLIT, capacity, D).astype(jnp.float32), axis=1
    )
    expert_rows = summed.astype(jnp.bfloat16).reshape(experts_count * capacity, D)
    picked = jnp.take(expert_rows, target, axis=0).reshape(rows_dev, 2, D)
    gate_scale = gate_fixed.astype(jnp.float32) / 1024.0
    mixture = jnp.sum(picked.astype(jnp.float32) * gate_scale[:, :, None], axis=1)
    return (attended.astype(jnp.float32) + modulation[2] * mixture).astype(jnp.bfloat16)


def shards(queries, key_rows, values, modulation, expert_in, expert_out, routes, gate_fixed):
    attended, normed = attention(queries, key_rows, values, modulation)
    n = lax.axis_size("tile")
    cap = 3 * queries.shape[0] // (n // SPLIT)
    fits = cap % 16 == 0 and kernel_bytes(n, cap, expert_in.shape[1]) < VMEM_LIMIT * 3 // 4
    experts = experts_kernel if fits else experts_sparse
    return experts(normed, attended, modulation, expert_in, expert_out, routes, gate_fixed)


def solution(mesh):
    placed = (
        P(("groups", "tile"), None),
        P(("groups", "tile"), None),
        P(("groups", "tile"), None),
        P("groups", None),
        P(None, "tile"),
        P("tile", None),
        P(("groups", "tile"), None),
        P(("groups", "tile"), None),
    )
    return jax.shard_map(
        shards, mesh=mesh, in_specs=placed, out_specs=P(("groups", "tile"), None), check_vma=False
    )
```

```python
import functools
import math

import jax
import jax.numpy as jnp
from jax import lax
from jax.experimental import pallas as pl
from jax.experimental.pallas import tpu as pltpu
from jax.sharding import PartitionSpec as P

HEAD_DIM = 128
D = 4096
SPLIT = 4
TILE_COLS = 8

EPSILON = 1e-06
MASKED = -1e30
MESH = pl.DeviceIdType.MESH
VMEM_LIMIT = 60 * 1024 * 1024


def when(cond, body):
    if cond is True:
        body()
    else:
        pl.when(cond)(body)


def both(a, b):
    if a is True:
        return b
    if b is True:
        return a
    return jnp.logical_and(a, b)


def remote(src, dst, send_sem, recv_sem, target):
    return pltpu.make_async_remote_copy(
        src_ref=src,
        dst_ref=dst,
        send_sem=send_sem,
        recv_sem=recv_sem,
        device_id={"tile": target},
        device_id_type=MESH,
    )


def halo_levels(n):
    grid_rows = n // TILE_COLS
    if grid_rows < 2:
        return 1
    return 2 if grid_rows == 2 else 3


def attention_kernel(
    n, rows, q_ref, k_ref, v_ref, mod_ref, att_ref, norm_ref, keys, vals, send_sem, recv_sem, own_sem
):
    me = lax.axis_index("tile")
    grid_rows = n // TILE_COLS
    tile = lax.rem(me + TILE_COLS // 2, n)
    row = lax.div(tile, TILE_COLS)
    col = lax.rem(tile, TILE_COLS)
    if grid_rows < 2:
        verticals = []
    elif grid_rows == 2:
        verticals = [(1, TILE_COLS, True, 1)]
    else:
        verticals = [(1, n - TILE_COLS, row > 0, 2), (2, TILE_COLS, row < grid_rows - 1, 1)]
    sides = [(-1, col > 0), (1, col < TILE_COLS - 1)]
    here = {level: exists for level, _, exists, _ in verticals}
    here[0] = True

    def slot(level, side):
        return level * 3 + 1 + side

    def place(buf, s):
        return buf.at[pl.ds(s * rows, rows), :]

    def over(offset):
        return lax.rem(me + offset + n, n)

    half = rows // 2
    middle = TILE_COLS // 2
    crossing = {side: col == (middle if side < 0 else middle - 1) for side, _ in sides}
    two = grid_rows == 2

    def part_of(buf, s, h):
        return buf.at[pl.ds(pl.multiple_of(s * rows + h * half, half), half), :]

    own = [
        pltpu.make_async_copy(src, place(buf, slot(0, 0)), own_sem.at[i])
        for i, (src, buf) in enumerate(((k_ref, keys), (v_ref, vals)))
    ]
    for copy in own:
        copy.start()

    def beside(side):
        if not two:
            return over(side)
        return jnp.where(crossing[side], over(side + TILE_COLS), over(side))

    def level_there(level, side):
        return jnp.where(crossing[side], 1 - level, level) if two else level

    barrier = pltpu.get_barrier_semaphore()
    partners = [(over(offset), exists) for _, offset, exists, _ in verticals]
    partners += [(beside(side), exists) for side, exists in sides]
    for target, exists in partners:

        def greet(target=target):
            pl.semaphore_signal(barrier, inc=1, device_id={"tile": target}, device_id_type=MESH)

        when(exists, greet)
    expected = sum(1 if exists is True else jnp.where(exists, 1, 0) for _, exists in partners)
    pl.semaphore_wait(barrier, expected)

    sends = []
    pieces = [(i, h) for i in (0, 1) for h in (0, 1)]
    bufs = (keys, vals)

    def push(i, h, src, there, target, exists):
        copy = remote(
            src,
            part_of(bufs[i], there, h),
            send_sem.at[len(sends)],
            recv_sem.at[there, i * 2 + h],
            target,
        )
        when(exists, copy.start)
        sends.append((copy, exists))

    def arrived(s, exists, i, h):
        ref = part_of(bufs[i], s, h)
        when(exists, remote(ref, ref, send_sem.at[0], recv_sem.at[s, i * 2 + h], me).wait_recv)

    def own_part(i, h):
        return (k_ref, v_ref)[i].at[pl.ds(h * half, half), :]

    for i, h in pieces:
        for level, offset, exists, there in verticals:
            push(i, h, own_part(i, h), slot(there, 0), over(offset), exists)
    for i, h in pieces:
        for side, exists in sides:
            push(i, h, own_part(i, h), slot(level_there(0, side), -side), beside(side), exists)
    for s in range(3 * (1 + len(verticals))):
        level, side = s // 3, s % 3 - 1
        exists = here[level]
        for other, side_exists in sides:
            if other == side:
                exists = both(exists, side_exists)
        if exists is True:
            continue

        def clear(s=s):
            for buf in (keys, vals):
                buf[pl.ds(s * rows, rows), :] = jnp.zeros((rows, D), buf.dtype)

        pl.when(jnp.logical_not(exists))(clear)
    for i, h in pieces:
        for level, offset, exists, there in verticals:
            arrived(slot(level, 0), exists, i, h)
            for side, side_exists in sides:
                push(
                    i,
                    h,
                    part_of(bufs[i], slot(level, 0), h),
                    slot(level_there(level, side), -side),
                    beside(side),
                    both(exists, side_exists),
                )
    for copy in own:
        copy.wait()
    for i, h in pieces:
        for level, exists in sorted(here.items(), key=lambda item: item[0]):
            for side, side_exists in sides:
                arrived(slot(level, side), both(exists, side_exists), i, h)

    span = 3 * (1 + len(verticals)) * rows
    where = lax.broadcasted_iota(jnp.int32, (rows, span), 1)
    bias = jnp.zeros((rows, span), jnp.float32)
    for s in range(span // rows):
        level, side = s // 3, s % 3 - 1
        exists = here[level]
        for other, side_exists in sides:
            if other == side:
                exists = both(exists, side_exists)
        if exists is True:
            continue
        penalty = jnp.where(exists, 0.0, MASKED)
        bias = jnp.where((where >= s * rows) & (where < (s + 1) * rows), penalty, bias)
    scale = 1.0 / math.sqrt(HEAD_DIM)
    together = 4

    def heads(step, carry):
        for extra in range(together):
            at = pl.ds(pl.multiple_of((step * together + extra) * HEAD_DIM, HEAD_DIM), HEAD_DIM)
            scores = lax.dot_general(
                q_ref[:, at], keys[:, at], (((1,), (1,)), ((), ())), preferred_element_type=jnp.float32
            )
            scores = scores * scale + bias
            raised = jnp.exp(scores - jnp.max(scores, axis=-1, keepdims=True))
            probs = (raised * (1.0 / jnp.sum(raised, axis=-1, keepdims=True))).astype(jnp.bfloat16)
            att_ref[:, at] = jnp.dot(probs, vals[:, at], preferred_element_type=jnp.float32).astype(
                att_ref.dtype
            )
        return carry

    lax.fori_loop(0, D // HEAD_DIM // together, heads, 0)

    def normalise(step, carry):
        at = pl.ds(pl.multiple_of(step * 16, 16), 16)
        wide = att_ref[at, :].astype(jnp.float32)
        wide = wide - jnp.mean(wide, axis=-1, keepdims=True)
        spread = jnp.mean(wide * wide, axis=-1, keepdims=True)
        normed = wide * lax.rsqrt(spread + EPSILON)
        norm_ref[at, :] = (normed * (1.0 + mod_ref[1:2, :]) + mod_ref[0:1, :]).astype(norm_ref.dtype)
        return carry

    lax.fori_loop(0, rows // 16, normalise, 0)
    for copy, exists in sends:
        when(exists, copy.wait_send)


def attention(queries, key_rows, values, modulation):
    n = lax.axis_size("tile")
    rows = queries.shape[0]
    levels = halo_levels(n)
    slots = 3 * levels
    vmem = pl.BlockSpec(memory_space=pltpu.VMEM)
    hbm = pl.BlockSpec(memory_space=pl.ANY)
    return pl.pallas_call(
        functools.partial(attention_kernel, n, rows),
        name="halo_attention",
        out_shape=(
            jax.ShapeDtypeStruct((rows, D), jnp.bfloat16),
            jax.ShapeDtypeStruct((rows, D), jnp.bfloat16),
        ),
        in_specs=[vmem, hbm, hbm, vmem],
        out_specs=(vmem, vmem),
        scratch_shapes=[
            pltpu.VMEM((slots * rows, D), jnp.bfloat16),
            pltpu.VMEM((slots * rows, D), jnp.bfloat16),
            pltpu.SemaphoreType.DMA((4 * (2 + 3 * (levels - 1)),)),
            pltpu.SemaphoreType.DMA((slots, 4)),
            pltpu.SemaphoreType.DMA((2,)),
        ],
        compiler_params=pltpu.CompilerParams(
            collective_id=0, has_side_effects=True, vmem_limit_bytes=VMEM_LIMIT
        ),
    )(queries, key_rows, values, modulation)


def nearest_first(p, planes):
    order = [p] + [p * 0] * (planes - 1)
    count = p * 0 + 1
    for step in range(1, planes):
        for other in (p - step, p + step):
            exists = jnp.logical_and(other >= 0, other < planes)
            for i in range(1, planes):
                order[i] = jnp.where(jnp.logical_and(exists, count == i), other, order[i])
            count = count + jnp.where(exists, 1, 0)
    return order


def expert_kernel(
    n, rows, cap, slots_ref, att_ref, mod_ref, high_ref, low_ref, first_ref, second_ref, out_ref,
    tokens, first, second, hidden, part, r1, r2, r3,
    send_sem, token_sem, s1_sem, s2_sem, s3_sem, own_sem,
):
    planes = n // SPLIT
    width = first_ref.shape[1]
    me = lax.axis_index("tile")
    p = lax.div(me, SPLIT)
    q = lax.rem(me, SPLIT)
    y = lax.div(q, 2)
    c = lax.rem(q, 2)
    plane_of = nearest_first(p, planes)

    def device(plane, yy, cc):
        return plane * SPLIT + yy * 2 + cc

    beside = device(p, 1 - y, c)
    twin = device(p, y, 1 - c)

    def block(buf, index):
        return buf.at[pl.ds(pl.multiple_of(index * cap, 16), cap), :]

    loads = [
        pltpu.make_async_copy(block(slots_ref, p), block(tokens, me), own_sem.at[0]),
        pltpu.make_async_copy(first_ref, first, own_sem.at[1]),
        pltpu.make_async_copy(second_ref, second, own_sem.at[2]),
    ]
    for load in loads:
        load.start()

    barrier = pltpu.get_barrier_semaphore()
    targets = [beside, twin] + [device(plane, y, c) for plane in plane_of[1:]]
    for target in targets:
        pl.semaphore_signal(barrier, inc=1, device_id={"tile": target}, device_id_type=MESH)
    pl.semaphore_wait(barrier, len(targets))

    sends = []

    def push(src, dst, recv, target):
        copy = remote(src, dst, send_sem.at[len(sends)], recv, target)
        copy.start()
        sends.append(copy)

    def landed(dst, recv):
        remote(dst, dst, send_sem.at[0], recv, me).wait_recv()

    def give(tile, target):
        push(block(tokens, tile), block(tokens, tile), token_sem.at[tile], target)

    def take(tile):
        landed(block(tokens, tile), token_sem.at[tile])

    for target in (beside, twin):
        push(block(slots_ref, p), block(tokens, me), token_sem.at[me], target)
    for plane in plane_of[1:]:
        push(block(slots_ref, plane), block(tokens, me), token_sem.at[me], device(plane, y, c))

    def forward(i, cond=True, copies=None):
        tile = device(plane_of[i], y, c)
        if copies is None:
            copies = []
            for target in (beside, twin):
                ref = block(tokens, tile)
                copies.append(remote(ref, ref, send_sem.at[len(sends)], token_sem.at[tile], target))
                sends.append(copies[-1])

        def go():
            take(tile)
            for copy in copies:
                copy.start()

        when(cond, go)
        return copies

    def forward_more(i):
        tile = device(plane_of[i], 1 - y, c)
        take(tile)
        give(tile, twin)

    group = SPLIT * cap
    chunk = min(width, 256)
    chunk_out = 512

    def compute(i):
        plane = plane_of[i]
        for yy in (0, 1):
            take(device(plane, yy, 1 - c))
        at = pl.ds(pl.multiple_of(plane * group, 16), group)

        def one(step, carry):
            cols = pl.ds(pl.multiple_of(step * chunk, chunk), chunk)
            raw = jnp.dot(tokens[at, :], first[:, cols], preferred_element_type=jnp.float32)
            hidden[:, cols] = jax.nn.gelu(raw, approximate=True).astype(hidden.dtype)
            return carry

        lax.fori_loop(0, width // chunk, one, 0)

        def two(step, carry):
            cols = pl.ds(pl.multiple_of(step * chunk_out, chunk_out), chunk_out)
            raw = jnp.dot(hidden[...], second[:, cols], preferred_element_type=jnp.float32)
            part[at, cols] = raw.astype(part.dtype)
            return carry

        lax.fori_loop(0, D // chunk_out, two, 0)
        for yy in (0, 1):
            push(
                block(part, device(plane, yy, 1 - c)),
                block(r1, plane * 2 + yy),
                s1_sem.at[plane, yy],
                twin,
            )

    def add(tile, other, index):
        def body(step, carry):
            at = pl.ds(pl.multiple_of(tile * cap + step * 16, 16), 16)
            extra = other[pl.ds(pl.multiple_of(index * cap + step * 16, 16), 16), :]
            part[at, :] = (part[at, :].astype(jnp.float32) + extra.astype(jnp.float32)).astype(part.dtype)
            return carry

        lax.fori_loop(0, cap // 16, body, 0)

    def fold_twin(i):
        plane = plane_of[i]
        for yy in (1 - y, y):
            landed(block(r1, plane * 2 + yy), s1_sem.at[plane, yy])
            add(device(plane, yy, c), r1, plane * 2 + yy)
            if yy is not y:
                push(block(part, device(plane, yy, c)), block(r2, plane), s2_sem.at[plane], beside)

    def fold_beside(i):
        plane = plane_of[i]
        landed(block(r2, plane), s2_sem.at[plane])
        tile = device(plane, y, c)
        if i == 0:

            def body(step, carry):
                at = pl.ds(pl.multiple_of(p * cap + step * 16, 16), 16)
                mine = part[pl.ds(pl.multiple_of(me * cap + step * 16, 16), 16), :]
                r3[at, :] = (mine.astype(jnp.float32) + r2[at, :].astype(jnp.float32)).astype(r3.dtype)
                return carry

            lax.fori_loop(0, cap // 16, body, 0)
        else:
            add(tile, r2, plane)
            push(block(part, tile), block(r3, p), s3_sem.at[p], tile)

    loads[0].wait()
    take(beside)
    give(beside, twin)
    for load in loads[1:]:
        load.wait()
    inner = jnp.logical_and(p > 0, p < planes - 1)
    if planes > 1:
        forward(1)
    if planes > 2:
        early = forward(2, inner)
    compute(0)
    fold_twin(0)
    for i in range(1, planes):
        forward_more(i)
        if i >= 2 and i + 1 < planes:
            forward(i + 1)
        compute(i)
        fold_twin(i)
        fold_beside(i - 1)
        if i == 1 and planes > 2:
            forward(2, jnp.logical_not(inner), early)
    fold_beside(planes - 1)
    for plane in plane_of[1:]:
        landed(block(r3, plane), s3_sem.at[plane])

    def finish(step, carry):
        cols = pl.ds(pl.multiple_of(step * chunk_out, chunk_out), chunk_out)
        found = r3[:, cols]
        mixture = jnp.dot(high_ref[...], found, preferred_element_type=jnp.float32)
        mixture = mixture + jnp.dot(low_ref[...], found, preferred_element_type=jnp.float32)
        out_ref[:, cols] = (
            att_ref[:, cols].astype(jnp.float32) + mod_ref[2:3, cols] * mixture
        ).astype(out_ref.dtype)
        return carry

    lax.fori_loop(0, D // chunk_out, finish, 0)
    for copy in sends:
        copy.wait_send()


def kernel_bytes(n, cap, width):
    planes = n // SPLIT
    lines = 2 * n * cap + planes * 4 * cap
    return 2 * (lines * D + 2 * width * D)


def experts_kernel(normed, attended, modulation, expert_in, expert_out, routes, gate_fixed):
    n = lax.axis_size("tile")
    rows = normed.shape[0]
    width = expert_in.shape[1]
    planes = n // SPLIT
    cap = 3 * rows // planes
    flat = routes.reshape(-1)
    target = flat * cap + slot_table(flat, planes)
    hit = (target[None, :] == jnp.arange(planes * cap, dtype=jnp.int32)[:, None]).astype(jnp.float32)
    chooser = hit.reshape(planes * cap, rows, 2).sum(axis=2).astype(jnp.bfloat16)
    gates = (hit * (gate_fixed.reshape(-1).astype(jnp.float32) / 1024.0)[None, :]).reshape(
        planes * cap, rows, 2
    ).sum(axis=2).T
    coarse = jnp.floor(gates * 128.0) / 128.0
    high = coarse.astype(jnp.bfloat16)
    low = (gates - coarse).astype(jnp.bfloat16)
    slots = jnp.dot(chooser, normed, preferred_element_type=jnp.float32).astype(jnp.bfloat16)
    vmem = pl.BlockSpec(memory_space=pltpu.VMEM)
    hbm = pl.BlockSpec(memory_space=pl.ANY)
    dma = pltpu.SemaphoreType.DMA
    count_sends = 8 * planes + 8
    bf = jnp.bfloat16
    return pl.pallas_call(
        functools.partial(expert_kernel, n, rows, cap),
        name="routed_experts",
        out_shape=jax.ShapeDtypeStruct((rows, D), bf),
        in_specs=[hbm, vmem, vmem, vmem, vmem, hbm, hbm],
        out_specs=vmem,
        scratch_shapes=[
            pltpu.VMEM((n * cap, D), bf),
            pltpu.VMEM((D, width), bf),
            pltpu.VMEM((width, D), bf),
            pltpu.VMEM((SPLIT * cap, width), bf),
            pltpu.VMEM((n * cap, D), bf),
            pltpu.VMEM((planes * 2 * cap, D), bf),
            pltpu.VMEM((planes * cap, D), bf),
            pltpu.VMEM((planes * cap, D), bf),
            dma((count_sends,)),
            dma((n,)),
            dma((planes, 2)),
            dma((planes,)),
            dma((planes,)),
            dma((3,)),
        ],
        compiler_params=pltpu.CompilerParams(
            collective_id=1, has_side_effects=True, vmem_limit_bytes=VMEM_LIMIT
        ),
    )(slots, attended, modulation, high, low, expert_in, expert_out)


def slot_table(flat, experts_count):
    onehot = (flat[:, None] == jnp.arange(experts_count, dtype=jnp.int32)[None, :]).astype(
        jnp.int32
    )
    before = jnp.cumsum(onehot, axis=0) - onehot
    return jnp.sum(before * onehot, axis=1)


def expert_apply(rows, first_weight, second_weight):
    hidden = jax.nn.gelu(
        jnp.dot(rows, first_weight, preferred_element_type=jnp.float32), approximate=True
    ).astype(jnp.bfloat16)
    return jnp.dot(hidden, second_weight, preferred_element_type=jnp.float32).astype(jnp.bfloat16)


def experts_sparse(normed, attended, modulation, expert_in, expert_out, routes, gate_fixed):
    devices = lax.axis_size("tile")
    rows_dev = normed.shape[0]
    experts_count = devices // SPLIT
    capacity = 3 * rows_dev // experts_count
    flat = routes.reshape(-1)
    slots = slot_table(flat, experts_count)
    target = flat * capacity + slots
    chooser = (
        target[None, :] == jnp.arange(experts_count * capacity, dtype=jnp.int32)[:, None]
    ).astype(jnp.bfloat16)
    chooser = chooser.reshape(experts_count * capacity, rows_dev, 2).sum(axis=2)
    buffer = jnp.dot(chooser, normed, preferred_element_type=jnp.float32).astype(jnp.bfloat16)
    copies = jnp.broadcast_to(
        buffer.reshape(experts_count, 1, capacity, D), (experts_count, SPLIT, capacity, D)
    ).reshape(devices, capacity, D)
    received = lax.all_to_all(copies, "tile", split_axis=0, concat_axis=0, tiled=True)
    sources = received.shape[0]
    count = received.shape[1]
    partial_value = expert_apply(received.reshape(sources * count, D), expert_in, expert_out)
    returned = lax.all_to_all(
        partial_value.reshape(sources, count, D), "tile", split_axis=0, concat_axis=0, tiled=True
    )
    summed = jnp.sum(
        returned.reshape(experts_count, SPLIT, capacity, D).astype(jnp.float32), axis=1
    )
    expert_rows = summed.astype(jnp.bfloat16).reshape(experts_count * capacity, D)
    picked = jnp.take(expert_rows, target, axis=0).reshape(rows_dev, 2, D)
    gate_scale = gate_fixed.astype(jnp.float32) / 1024.0
    mixture = jnp.sum(picked.astype(jnp.float32) * gate_scale[:, :, None], axis=1)
    return (attended.astype(jnp.float32) + modulation[2] * mixture).astype(jnp.bfloat16)


def shards(queries, key_rows, values, modulation, expert_in, expert_out, routes, gate_fixed):
    attended, normed = attention(queries, key_rows, values, modulation)
    n = lax.axis_size("tile")
    cap = 3 * queries.shape[0] // (n // SPLIT)
    fits = cap % 16 == 0 and kernel_bytes(n, cap, expert_in.shape[1]) < VMEM_LIMIT * 3 // 4
    experts = experts_kernel if fits else experts_sparse
    return experts(normed, attended, modulation, expert_in, expert_out, routes, gate_fixed)


def solution(mesh):
    placed = (
        P(("groups", "tile"), None),
        P(("groups", "tile"), None),
        P(("groups", "tile"), None),
        P("groups", None),
        P(None, "tile"),
        P("tile", None),
        P(("groups", "tile"), None),
        P(("groups", "tile"), None),
    )
    return jax.shard_map(
        shards, mesh=mesh, in_specs=placed, out_specs=P(("groups", "tile"), None), check_vma=False
    )
```

```python
import functools
import math

import jax
import jax.numpy as jnp
from jax import lax
from jax.experimental import pallas as pl
from jax.experimental.pallas import tpu as pltpu
from jax.sharding import PartitionSpec as P

HEAD_DIM = 128
D = 4096
SPLIT = 4
TILE_COLS = 8

EPSILON = 1e-06
MASKED = -1e30
MESH = pl.DeviceIdType.MESH
VMEM_LIMIT = 60 * 1024 * 1024


def when(cond, body):
    if cond is True:
        body()
    else:
        pl.when(cond)(body)


def both(a, b):
    if a is True:
        return b
    if b is True:
        return a
    return jnp.logical_and(a, b)


def remote(src, dst, send_sem, recv_sem, target):
    return pltpu.make_async_remote_copy(
        src_ref=src,
        dst_ref=dst,
        send_sem=send_sem,
        recv_sem=recv_sem,
        device_id={"tile": target},
        device_id_type=MESH,
    )


def halo_levels(n):
    grid_rows = n // TILE_COLS
    if grid_rows < 2:
        return 1
    return 2 if grid_rows == 2 else 3


def attention_kernel(
    n, rows, q_ref, k_ref, v_ref, mod_ref, att_ref, norm_ref, keys, vals, send_sem, recv_sem, own_sem,
    also=None,
):
    me = lax.axis_index("tile")
    grid_rows = n // TILE_COLS
    tile = lax.rem(me + TILE_COLS // 2, n)
    row = lax.div(tile, TILE_COLS)
    col = lax.rem(tile, TILE_COLS)
    if grid_rows < 2:
        verticals = []
    elif grid_rows == 2:
        verticals = [(1, TILE_COLS, True, 1)]
    else:
        verticals = [(1, n - TILE_COLS, row > 0, 2), (2, TILE_COLS, row < grid_rows - 1, 1)]
    sides = [(-1, col > 0), (1, col < TILE_COLS - 1)]
    here = {level: exists for level, _, exists, _ in verticals}
    here[0] = True

    def slot(level, side):
        return level * 3 + 1 + side

    def place(buf, s):
        return buf.at[pl.ds(s * rows, rows), :]

    def over(offset):
        return lax.rem(me + offset + n, n)

    half = rows // 2
    middle = TILE_COLS // 2
    crossing = {side: col == (middle if side < 0 else middle - 1) for side, _ in sides}
    two = grid_rows == 2

    def part_of(buf, s, h):
        return buf.at[pl.ds(pl.multiple_of(s * rows + h * half, half), half), :]

    own = [
        pltpu.make_async_copy(src, place(buf, slot(0, 0)), own_sem.at[i])
        for i, (src, buf) in enumerate(((k_ref, keys), (v_ref, vals)))
    ]
    for copy in own:
        copy.start()

    def beside(side):
        if not two:
            return over(side)
        return jnp.where(crossing[side], over(side + TILE_COLS), over(side))

    def level_there(level, side):
        return jnp.where(crossing[side], 1 - level, level) if two else level

    barrier = pltpu.get_barrier_semaphore()
    partners = [(over(offset), exists) for _, offset, exists, _ in verticals]
    partners += [(beside(side), exists) for side, exists in sides]
    partners += [(target, True) for target in also or []]
    for target, exists in partners:

        def greet(target=target):
            pl.semaphore_signal(barrier, inc=1, device_id={"tile": target}, device_id_type=MESH)

        when(exists, greet)
    expected = sum(1 if exists is True else jnp.where(exists, 1, 0) for _, exists in partners)
    pl.semaphore_wait(barrier, expected)

    sends = []
    pieces = [(i, h) for i in (0, 1) for h in (0, 1)]
    bufs = (keys, vals)

    def push(i, h, src, there, target, exists):
        copy = remote(
            src,
            part_of(bufs[i], there, h),
            send_sem.at[len(sends)],
            recv_sem.at[there, i * 2 + h],
            target,
        )
        when(exists, copy.start)
        sends.append((copy, exists))

    def arrived(s, exists, i, h):
        ref = part_of(bufs[i], s, h)
        when(exists, remote(ref, ref, send_sem.at[0], recv_sem.at[s, i * 2 + h], me).wait_recv)

    def own_part(i, h):
        return (k_ref, v_ref)[i].at[pl.ds(h * half, half), :]

    for i, h in pieces:
        for level, offset, exists, there in verticals:
            push(i, h, own_part(i, h), slot(there, 0), over(offset), exists)
    for i, h in pieces:
        for side, exists in sides:
            push(i, h, own_part(i, h), slot(level_there(0, side), -side), beside(side), exists)
    for s in range(3 * (1 + len(verticals))):
        level, side = s // 3, s % 3 - 1
        exists = here[level]
        for other, side_exists in sides:
            if other == side:
                exists = both(exists, side_exists)
        if exists is True:
            continue

        def clear(s=s):
            for buf in (keys, vals):
                buf[pl.ds(s * rows, rows), :] = jnp.zeros((rows, D), buf.dtype)

        pl.when(jnp.logical_not(exists))(clear)
    for i, h in pieces:
        for level, offset, exists, there in verticals:
            arrived(slot(level, 0), exists, i, h)
            for side, side_exists in sides:
                push(
                    i,
                    h,
                    part_of(bufs[i], slot(level, 0), h),
                    slot(level_there(level, side), -side),
                    beside(side),
                    both(exists, side_exists),
                )
    for copy in own:
        copy.wait()
    for i, h in pieces:
        for level, exists in sorted(here.items(), key=lambda item: item[0]):
            for side, side_exists in sides:
                arrived(slot(level, side), both(exists, side_exists), i, h)

    span = 3 * (1 + len(verticals)) * rows
    where = lax.broadcasted_iota(jnp.int32, (rows, span), 1)
    bias = jnp.zeros((rows, span), jnp.float32)
    for s in range(span // rows):
        level, side = s // 3, s % 3 - 1
        exists = here[level]
        for other, side_exists in sides:
            if other == side:
                exists = both(exists, side_exists)
        if exists is True:
            continue
        penalty = jnp.where(exists, 0.0, MASKED)
        bias = jnp.where((where >= s * rows) & (where < (s + 1) * rows), penalty, bias)
    scale = 1.0 / math.sqrt(HEAD_DIM)
    together = 4

    def heads(step, carry):
        for extra in range(together):
            at = pl.ds(pl.multiple_of((step * together + extra) * HEAD_DIM, HEAD_DIM), HEAD_DIM)
            scores = lax.dot_general(
                q_ref[:, at], keys[:, at], (((1,), (1,)), ((), ())), preferred_element_type=jnp.float32
            )
            scores = scores * scale + bias
            raised = jnp.exp(scores - jnp.max(scores, axis=-1, keepdims=True))
            probs = (raised * (1.0 / jnp.sum(raised, axis=-1, keepdims=True))).astype(jnp.bfloat16)
            att_ref[:, at] = jnp.dot(probs, vals[:, at], preferred_element_type=jnp.float32).astype(
                att_ref.dtype
            )
        return carry

    lax.fori_loop(0, D // HEAD_DIM // together, heads, 0)

    def normalise(step, carry):
        at = pl.ds(pl.multiple_of(step * 16, 16), 16)
        wide = att_ref[at, :].astype(jnp.float32)
        wide = wide - jnp.mean(wide, axis=-1, keepdims=True)
        spread = jnp.mean(wide * wide, axis=-1, keepdims=True)
        normed = wide * lax.rsqrt(spread + EPSILON)
        norm_ref[at, :] = (normed * (1.0 + mod_ref[1:2, :]) + mod_ref[0:1, :]).astype(norm_ref.dtype)
        return carry

    lax.fori_loop(0, rows // 16, normalise, 0)
    if also is not None:
        return sends
    for copy, exists in sends:
        when(exists, copy.wait_send)


def attention(queries, key_rows, values, modulation):
    n = lax.axis_size("tile")
    rows = queries.shape[0]
    levels = halo_levels(n)
    slots = 3 * levels
    vmem = pl.BlockSpec(memory_space=pltpu.VMEM)
    hbm = pl.BlockSpec(memory_space=pl.ANY)
    return pl.pallas_call(
        functools.partial(attention_kernel, n, rows),
        name="halo_attention",
        out_shape=(
            jax.ShapeDtypeStruct((rows, D), jnp.bfloat16),
            jax.ShapeDtypeStruct((rows, D), jnp.bfloat16),
        ),
        in_specs=[vmem, hbm, hbm, vmem],
        out_specs=(vmem, vmem),
        scratch_shapes=[
            pltpu.VMEM((slots * rows, D), jnp.bfloat16),
            pltpu.VMEM((slots * rows, D), jnp.bfloat16),
            pltpu.SemaphoreType.DMA((4 * (2 + 3 * (levels - 1)),)),
            pltpu.SemaphoreType.DMA((slots, 4)),
            pltpu.SemaphoreType.DMA((2,)),
        ],
        compiler_params=pltpu.CompilerParams(
            collective_id=0, has_side_effects=True, vmem_limit_bytes=VMEM_LIMIT
        ),
    )(queries, key_rows, values, modulation)


def nearest_first(p, planes):
    order = [p] + [p * 0] * (planes - 1)
    count = p * 0 + 1
    for step in range(1, planes):
        for other in (p - step, p + step):
            exists = jnp.logical_and(other >= 0, other < planes)
            for i in range(1, planes):
                order[i] = jnp.where(jnp.logical_and(exists, count == i), other, order[i])
            count = count + jnp.where(exists, 1, 0)
    return order


def positions(n):
    me = lax.axis_index("tile")
    p = lax.div(me, SPLIT)
    q = lax.rem(me, SPLIT)
    return me, p, lax.div(q, 2), lax.rem(q, 2), nearest_first(p, n // SPLIT)


def device(plane, yy, cc):
    return plane * SPLIT + yy * 2 + cc


def layer_kernel(
    n, rows, cap, q_ref, k_ref, v_ref, mod_ref, chooser_ref, high_ref, low_ref, first_ref, second_ref,
    out_ref, att, norm, slots, keys, vals, halo_send, halo_recv, halo_own,
    tokens, first, second, hidden, part, r1, r2, r3,
    send_sem, token_sem, s1_sem, s2_sem, s3_sem, own_sem,
):
    me, p, y, c, plane_of = positions(n)
    loads = [
        pltpu.make_async_copy(first_ref, first, own_sem.at[1]),
        pltpu.make_async_copy(second_ref, second, own_sem.at[2]),
    ]
    for load in loads:
        load.start()
    targets = [device(p, 1 - y, c), device(p, y, 1 - c)]
    targets += [device(plane, y, c) for plane in plane_of[1:]]
    pending = attention_kernel(
        n, rows, q_ref, k_ref, v_ref, mod_ref, att, norm, keys, vals, halo_send, halo_recv, halo_own,
        also=targets,
    )
    chunk = 512

    def pick(step, carry):
        cols = pl.ds(pl.multiple_of(step * chunk, chunk), chunk)
        slots[:, cols] = jnp.dot(
            chooser_ref[...], norm[:, cols], preferred_element_type=jnp.float32
        ).astype(slots.dtype)
        return carry

    lax.fori_loop(0, D // chunk, pick, 0)
    expert_part(
        n, cap, slots, att, mod_ref, high_ref, low_ref, loads, out_ref,
        tokens, first, second, hidden, part, r1, r2, r3,
        send_sem, token_sem, s1_sem, s2_sem, s3_sem, own_sem,
    )
    for copy, exists in pending:
        when(exists, copy.wait_send)


def expert_part(
    n, cap, slots_ref, att_ref, mod_ref, high_ref, low_ref, weights, out_ref,
    tokens, first, second, hidden, part, r1, r2, r3,
    send_sem, token_sem, s1_sem, s2_sem, s3_sem, own_sem,
):
    planes = n // SPLIT
    width = first.shape[1]
    me, p, y, c, plane_of = positions(n)
    beside = device(p, 1 - y, c)
    twin = device(p, y, 1 - c)

    def block(buf, index):
        return buf.at[pl.ds(pl.multiple_of(index * cap, 16), cap), :]

    mine = pltpu.make_async_copy(block(slots_ref, p), block(tokens, me), own_sem.at[0])
    mine.start()

    sends = []

    def push(src, dst, recv, target):
        copy = remote(src, dst, send_sem.at[len(sends)], recv, target)
        copy.start()
        sends.append(copy)

    def landed(dst, recv):
        remote(dst, dst, send_sem.at[0], recv, me).wait_recv()

    def give(tile, target):
        push(block(tokens, tile), block(tokens, tile), token_sem.at[tile], target)

    def take(tile):
        landed(block(tokens, tile), token_sem.at[tile])

    for target in (beside, twin):
        push(block(slots_ref, p), block(tokens, me), token_sem.at[me], target)
    for plane in plane_of[1:]:
        push(block(slots_ref, plane), block(tokens, me), token_sem.at[me], device(plane, y, c))

    def forward(i, cond=True, copies=None):
        tile = device(plane_of[i], y, c)
        if copies is None:
            copies = []
            for target in (beside, twin):
                ref = block(tokens, tile)
                copies.append(remote(ref, ref, send_sem.at[len(sends)], token_sem.at[tile], target))
                sends.append(copies[-1])

        def go():
            take(tile)
            for copy in copies:
                copy.start()

        when(cond, go)
        return copies

    def forward_more(i):
        tile = device(plane_of[i], 1 - y, c)
        take(tile)
        give(tile, twin)

    group = SPLIT * cap
    chunk = min(width, 256)
    chunk_out = 512

    def compute(i):
        plane = plane_of[i]
        for yy in (0, 1):
            take(device(plane, yy, 1 - c))
        at = pl.ds(pl.multiple_of(plane * group, 16), group)

        def one(step, carry):
            cols = pl.ds(pl.multiple_of(step * chunk, chunk), chunk)
            raw = jnp.dot(tokens[at, :], first[:, cols], preferred_element_type=jnp.float32)
            hidden[:, cols] = jax.nn.gelu(raw, approximate=True).astype(hidden.dtype)
            return carry

        lax.fori_loop(0, width // chunk, one, 0)

        def two(step, carry):
            cols = pl.ds(pl.multiple_of(step * chunk_out, chunk_out), chunk_out)
            raw = jnp.dot(hidden[...], second[:, cols], preferred_element_type=jnp.float32)
            part[at, cols] = raw.astype(part.dtype)
            return carry

        lax.fori_loop(0, D // chunk_out, two, 0)
        for yy in (0, 1):
            push(
                block(part, device(plane, yy, 1 - c)),
                block(r1, plane * 2 + yy),
                s1_sem.at[plane, yy],
                twin,
            )

    def add(tile, other, index):
        def body(step, carry):
            at = pl.ds(pl.multiple_of(tile * cap + step * 16, 16), 16)
            extra = other[pl.ds(pl.multiple_of(index * cap + step * 16, 16), 16), :]
            part[at, :] = (part[at, :].astype(jnp.float32) + extra.astype(jnp.float32)).astype(part.dtype)
            return carry

        lax.fori_loop(0, cap // 16, body, 0)

    def fold_twin(i):
        plane = plane_of[i]
        for yy in (1 - y, y):
            landed(block(r1, plane * 2 + yy), s1_sem.at[plane, yy])
            add(device(plane, yy, c), r1, plane * 2 + yy)
            if yy is not y:
                push(block(part, device(plane, yy, c)), block(r2, plane), s2_sem.at[plane], beside)

    def fold_beside(i):
        plane = plane_of[i]
        landed(block(r2, plane), s2_sem.at[plane])
        tile = device(plane, y, c)
        if i == 0:

            def body(step, carry):
                at = pl.ds(pl.multiple_of(p * cap + step * 16, 16), 16)
                own = part[pl.ds(pl.multiple_of(me * cap + step * 16, 16), 16), :]
                r3[at, :] = (own.astype(jnp.float32) + r2[at, :].astype(jnp.float32)).astype(r3.dtype)
                return carry

            lax.fori_loop(0, cap // 16, body, 0)
        else:
            add(tile, r2, plane)
            push(block(part, tile), block(r3, p), s3_sem.at[p], tile)

    mine.wait()
    take(beside)
    give(beside, twin)
    for load in weights:
        load.wait()
    inner = jnp.logical_and(p > 0, p < planes - 1)
    if planes > 1:
        forward(1)
    if planes > 2:
        early = forward(2, inner)
    compute(0)
    fold_twin(0)
    for i in range(1, planes):
        forward_more(i)
        if i >= 2 and i + 1 < planes:
            forward(i + 1)
        compute(i)
        fold_twin(i)
        fold_beside(i - 1)
        if i == 1 and planes > 2:
            forward(2, jnp.logical_not(inner), early)
    fold_beside(planes - 1)
    for plane in plane_of[1:]:
        landed(block(r3, plane), s3_sem.at[plane])

    def finish(step, carry):
        cols = pl.ds(pl.multiple_of(step * chunk_out, chunk_out), chunk_out)
        found = r3[:, cols]
        mixture = jnp.dot(high_ref[...], found, preferred_element_type=jnp.float32)
        mixture = mixture + jnp.dot(low_ref[...], found, preferred_element_type=jnp.float32)
        out_ref[:, cols] = (
            att_ref[:, cols].astype(jnp.float32) + mod_ref[2:3, cols] * mixture
        ).astype(out_ref.dtype)
        return carry

    lax.fori_loop(0, D // chunk_out, finish, 0)
    for copy in sends:
        copy.wait_send()


def kernel_bytes(n, cap, width):
    planes = n // SPLIT
    lines = 2 * n * cap + planes * 5 * cap + 2 * 3 * halo_levels(n) * cap * planes // 3
    return 2 * (lines * D + 2 * width * D)


def layer(queries, key_rows, values, modulation, expert_in, expert_out, routes, gate_fixed):
    n = lax.axis_size("tile")
    rows = queries.shape[0]
    width = expert_in.shape[1]
    planes = n // SPLIT
    cap = 3 * rows // planes
    flat = routes.reshape(-1)
    target = flat * cap + slot_table(flat, planes)
    hit = (target[None, :] == jnp.arange(planes * cap, dtype=jnp.int32)[:, None]).astype(jnp.float32)
    chooser = hit.reshape(planes * cap, rows, 2).sum(axis=2).astype(jnp.bfloat16)
    gates = (hit * (gate_fixed.reshape(-1).astype(jnp.float32) / 1024.0)[None, :]).reshape(
        planes * cap, rows, 2
    ).sum(axis=2).T
    coarse = jnp.floor(gates * 128.0) / 128.0
    high = coarse.astype(jnp.bfloat16)
    low = (gates - coarse).astype(jnp.bfloat16)
    levels = halo_levels(n)
    tiles = 3 * levels
    vmem = pl.BlockSpec(memory_space=pltpu.VMEM)
    hbm = pl.BlockSpec(memory_space=pl.ANY)
    dma = pltpu.SemaphoreType.DMA
    count_sends = 8 * planes + 8
    bf = jnp.bfloat16
    return pl.pallas_call(
        functools.partial(layer_kernel, n, rows, cap),
        name="whole_layer",
        out_shape=jax.ShapeDtypeStruct((rows, D), bf),
        in_specs=[vmem, hbm, hbm, vmem, vmem, vmem, vmem, hbm, hbm],
        out_specs=vmem,
        scratch_shapes=[
            pltpu.VMEM((rows, D), bf),
            pltpu.VMEM((rows, D), bf),
            pltpu.VMEM((planes * cap, D), bf),
            pltpu.VMEM((tiles * rows, D), bf),
            pltpu.VMEM((tiles * rows, D), bf),
            dma((4 * (2 + 3 * (levels - 1)),)),
            dma((tiles, 4)),
            dma((2,)),
            pltpu.VMEM((n * cap, D), bf),
            pltpu.VMEM((D, width), bf),
            pltpu.VMEM((width, D), bf),
            pltpu.VMEM((SPLIT * cap, width), bf),
            pltpu.VMEM((n * cap, D), bf),
            pltpu.VMEM((planes * 2 * cap, D), bf),
            pltpu.VMEM((planes * cap, D), bf),
            pltpu.VMEM((planes * cap, D), bf),
            dma((count_sends,)),
            dma((n,)),
            dma((planes, 2)),
            dma((planes,)),
            dma((planes,)),
            dma((3,)),
        ],
        compiler_params=pltpu.CompilerParams(
            collective_id=1, has_side_effects=True, vmem_limit_bytes=VMEM_LIMIT
        ),
    )(queries, key_rows, values, modulation, chooser, high, low, expert_in, expert_out)


def slot_table(flat, experts_count):
    onehot = (flat[:, None] == jnp.arange(experts_count, dtype=jnp.int32)[None, :]).astype(
        jnp.int32
    )
    before = jnp.cumsum(onehot, axis=0) - onehot
    return jnp.sum(before * onehot, axis=1)


def expert_apply(rows, first_weight, second_weight):
    hidden = jax.nn.gelu(
        jnp.dot(rows, first_weight, preferred_element_type=jnp.float32), approximate=True
    ).astype(jnp.bfloat16)
    return jnp.dot(hidden, second_weight, preferred_element_type=jnp.float32).astype(jnp.bfloat16)


def experts_sparse(normed, attended, modulation, expert_in, expert_out, routes, gate_fixed):
    devices = lax.axis_size("tile")
    rows_dev = normed.shape[0]
    experts_count = devices // SPLIT
    capacity = 3 * rows_dev // experts_count
    flat = routes.reshape(-1)
    slots = slot_table(flat, experts_count)
    target = flat * capacity + slots
    chooser = (
        target[None, :] == jnp.arange(experts_count * capacity, dtype=jnp.int32)[:, None]
    ).astype(jnp.bfloat16)
    chooser = chooser.reshape(experts_count * capacity, rows_dev, 2).sum(axis=2)
    buffer = jnp.dot(chooser, normed, preferred_element_type=jnp.float32).astype(jnp.bfloat16)
    copies = jnp.broadcast_to(
        buffer.reshape(experts_count, 1, capacity, D), (experts_count, SPLIT, capacity, D)
    ).reshape(devices, capacity, D)
    received = lax.all_to_all(copies, "tile", split_axis=0, concat_axis=0, tiled=True)
    sources = received.shape[0]
    count = received.shape[1]
    partial_value = expert_apply(received.reshape(sources * count, D), expert_in, expert_out)
    returned = lax.all_to_all(
        partial_value.reshape(sources, count, D), "tile", split_axis=0, concat_axis=0, tiled=True
    )
    summed = jnp.sum(
        returned.reshape(experts_count, SPLIT, capacity, D).astype(jnp.float32), axis=1
    )
    expert_rows = summed.astype(jnp.bfloat16).reshape(experts_count * capacity, D)
    picked = jnp.take(expert_rows, target, axis=0).reshape(rows_dev, 2, D)
    gate_scale = gate_fixed.astype(jnp.float32) / 1024.0
    mixture = jnp.sum(picked.astype(jnp.float32) * gate_scale[:, :, None], axis=1)
    return (attended.astype(jnp.float32) + modulation[2] * mixture).astype(jnp.bfloat16)


def shards(queries, key_rows, values, modulation, expert_in, expert_out, routes, gate_fixed):
    n = lax.axis_size("tile")
    cap = 3 * queries.shape[0] // (n // SPLIT)
    if cap % 16 == 0 and kernel_bytes(n, cap, expert_in.shape[1]) < VMEM_LIMIT * 3 // 4:
        return layer(queries, key_rows, values, modulation, expert_in, expert_out, routes, gate_fixed)
    attended, normed = attention(queries, key_rows, values, modulation)
    return experts_sparse(normed, attended, modulation, expert_in, expert_out, routes, gate_fixed)


def solution(mesh):
    placed = (
        P(("groups", "tile"), None),
        P(("groups", "tile"), None),
        P(("groups", "tile"), None),
        P("groups", None),
        P(None, "tile"),
        P("tile", None),
        P(("groups", "tile"), None),
        P(("groups", "tile"), None),
    )
    return jax.shard_map(
        shards, mesh=mesh, in_specs=placed, out_specs=P(("groups", "tile"), None), check_vma=False
    )
```

```python
import functools
import math

import jax
import jax.numpy as jnp
from jax import lax
from jax.experimental import pallas as pl
from jax.experimental.pallas import tpu as pltpu
from jax.sharding import PartitionSpec as P

HEAD_DIM = 128
D = 4096
SPLIT = 4
TILE_COLS = 8

EPSILON = 1e-06
MASKED = -1e30
MESH = pl.DeviceIdType.MESH
VMEM_LIMIT = 60 * 1024 * 1024


def when(cond, body):
    if cond is True:
        body()
    else:
        pl.when(cond)(body)


def both(a, b):
    if a is True:
        return b
    if b is True:
        return a
    return jnp.logical_and(a, b)


def remote(src, dst, send_sem, recv_sem, target):
    return pltpu.make_async_remote_copy(
        src_ref=src,
        dst_ref=dst,
        send_sem=send_sem,
        recv_sem=recv_sem,
        device_id={"tile": target},
        device_id_type=MESH,
    )


def halo_levels(n):
    grid_rows = n // TILE_COLS
    if grid_rows < 2:
        return 1
    return 2 if grid_rows == 2 else 3


def attention_kernel(
    n, rows, q_ref, k_ref, v_ref, mod_ref, att_ref, norm_ref, keys, vals, send_sem, recv_sem, own_sem,
    also=None,
):
    me = lax.axis_index("tile")
    grid_rows = n // TILE_COLS
    tile = lax.rem(me + TILE_COLS // 2, n)
    row = lax.div(tile, TILE_COLS)
    col = lax.rem(tile, TILE_COLS)
    if grid_rows < 2:
        verticals = []
    elif grid_rows == 2:
        verticals = [(1, TILE_COLS, True, 1)]
    else:
        verticals = [(1, n - TILE_COLS, row > 0, 2), (2, TILE_COLS, row < grid_rows - 1, 1)]
    sides = [(-1, col > 0), (1, col < TILE_COLS - 1)]
    here = {level: exists for level, _, exists, _ in verticals}
    here[0] = True

    def slot(level, side):
        return level * 3 + 1 + side

    def place(buf, s):
        return buf.at[pl.ds(s * rows, rows), :]

    def over(offset):
        return lax.rem(me + offset + n, n)

    half = rows // 2
    middle = TILE_COLS // 2
    crossing = {side: col == (middle if side < 0 else middle - 1) for side, _ in sides}
    two = grid_rows == 2

    def part_of(buf, s, h):
        return buf.at[pl.ds(pl.multiple_of(s * rows + h * half, half), half), :]

    own = [
        pltpu.make_async_copy(src, place(buf, slot(0, 0)), own_sem.at[i])
        for i, (src, buf) in enumerate(((k_ref, keys), (v_ref, vals)))
    ]
    for copy in own:
        copy.start()

    def beside(side):
        if not two:
            return over(side)
        return jnp.where(crossing[side], over(side + TILE_COLS), over(side))

    def level_there(level, side):
        return jnp.where(crossing[side], 1 - level, level) if two else level

    barrier = pltpu.get_barrier_semaphore()
    partners = [(over(offset), exists) for _, offset, exists, _ in verticals]
    partners += [(beside(side), exists) for side, exists in sides]
    partners += [(target, True) for target in also or []]
    for target, exists in partners:

        def greet(target=target):
            pl.semaphore_signal(barrier, inc=1, device_id={"tile": target}, device_id_type=MESH)

        when(exists, greet)
    expected = sum(1 if exists is True else jnp.where(exists, 1, 0) for _, exists in partners)
    pl.semaphore_wait(barrier, expected)

    sends = []
    pieces = [(i, h) for i in (0, 1) for h in (0, 1)]
    bufs = (keys, vals)

    def push(i, h, src, there, target, exists):
        copy = remote(
            src,
            part_of(bufs[i], there, h),
            send_sem.at[len(sends)],
            recv_sem.at[there, i * 2 + h],
            target,
        )
        when(exists, copy.start)
        sends.append((copy, exists))

    def arrived(s, exists, i, h):
        ref = part_of(bufs[i], s, h)
        when(exists, remote(ref, ref, send_sem.at[0], recv_sem.at[s, i * 2 + h], me).wait_recv)

    def own_part(i, h):
        return (k_ref, v_ref)[i].at[pl.ds(h * half, half), :]

    for i, h in pieces:
        for level, offset, exists, there in verticals:
            push(i, h, own_part(i, h), slot(there, 0), over(offset), exists)
    for i, h in pieces:
        for side, exists in sides:
            push(i, h, own_part(i, h), slot(level_there(0, side), -side), beside(side), exists)
    for s in range(3 * (1 + len(verticals))):
        level, side = s // 3, s % 3 - 1
        exists = here[level]
        for other, side_exists in sides:
            if other == side:
                exists = both(exists, side_exists)
        if exists is True:
            continue

        def clear(s=s):
            for buf in (keys, vals):
                buf[pl.ds(s * rows, rows), :] = jnp.zeros((rows, D), buf.dtype)

        pl.when(jnp.logical_not(exists))(clear)
    for i, h in pieces:
        for level, offset, exists, there in verticals:
            arrived(slot(level, 0), exists, i, h)
            for side, side_exists in sides:
                push(
                    i,
                    h,
                    part_of(bufs[i], slot(level, 0), h),
                    slot(level_there(level, side), -side),
                    beside(side),
                    both(exists, side_exists),
                )
    for copy in own:
        copy.wait()
    for i, h in pieces:
        for level, exists in sorted(here.items(), key=lambda item: item[0]):
            for side, side_exists in sides:
                arrived(slot(level, side), both(exists, side_exists), i, h)

    span = 3 * (1 + len(verticals)) * rows
    where = lax.broadcasted_iota(jnp.int32, (rows, span), 1)
    bias = jnp.zeros((rows, span), jnp.float32)
    for s in range(span // rows):
        level, side = s // 3, s % 3 - 1
        exists = here[level]
        for other, side_exists in sides:
            if other == side:
                exists = both(exists, side_exists)
        if exists is True:
            continue
        penalty = jnp.where(exists, 0.0, MASKED)
        bias = jnp.where((where >= s * rows) & (where < (s + 1) * rows), penalty, bias)
    scale = 1.0 / math.sqrt(HEAD_DIM)
    together = 8

    def heads(step, carry):
        for extra in range(together):
            at = pl.ds(pl.multiple_of((step * together + extra) * HEAD_DIM, HEAD_DIM), HEAD_DIM)
            scores = lax.dot_general(
                q_ref[:, at], keys[:, at], (((1,), (1,)), ((), ())), preferred_element_type=jnp.float32
            )
            scores = scores * scale + bias
            raised = jnp.exp(scores - jnp.max(scores, axis=-1, keepdims=True))
            probs = (raised * (1.0 / jnp.sum(raised, axis=-1, keepdims=True))).astype(jnp.bfloat16)
            att_ref[:, at] = jnp.dot(probs, vals[:, at], preferred_element_type=jnp.float32).astype(
                att_ref.dtype
            )
        return carry

    lax.fori_loop(0, D // HEAD_DIM // together, heads, 0)

    def normalise(step, carry):
        at = pl.ds(pl.multiple_of(step * 16, 16), 16)
        wide = att_ref[at, :].astype(jnp.float32)
        wide = wide - jnp.mean(wide, axis=-1, keepdims=True)
        spread = jnp.mean(wide * wide, axis=-1, keepdims=True)
        normed = wide * lax.rsqrt(spread + EPSILON)
        norm_ref[at, :] = (normed * (1.0 + mod_ref[1:2, :]) + mod_ref[0:1, :]).astype(norm_ref.dtype)
        return carry

    lax.fori_loop(0, rows // 16, normalise, 0)
    if also is not None:
        return sends
    for copy, exists in sends:
        when(exists, copy.wait_send)


def attention(queries, key_rows, values, modulation):
    n = lax.axis_size("tile")
    rows = queries.shape[0]
    levels = halo_levels(n)
    slots = 3 * levels
    vmem = pl.BlockSpec(memory_space=pltpu.VMEM)
    hbm = pl.BlockSpec(memory_space=pl.ANY)
    return pl.pallas_call(
        functools.partial(attention_kernel, n, rows),
        name="halo_attention",
        out_shape=(
            jax.ShapeDtypeStruct((rows, D), jnp.bfloat16),
            jax.ShapeDtypeStruct((rows, D), jnp.bfloat16),
        ),
        in_specs=[vmem, hbm, hbm, vmem],
        out_specs=(vmem, vmem),
        scratch_shapes=[
            pltpu.VMEM((slots * rows, D), jnp.bfloat16),
            pltpu.VMEM((slots * rows, D), jnp.bfloat16),
            pltpu.SemaphoreType.DMA((4 * (2 + 3 * (levels - 1)),)),
            pltpu.SemaphoreType.DMA((slots, 4)),
            pltpu.SemaphoreType.DMA((2,)),
        ],
        compiler_params=pltpu.CompilerParams(
            collective_id=0, has_side_effects=True, vmem_limit_bytes=VMEM_LIMIT
        ),
    )(queries, key_rows, values, modulation)


def nearest_first(p, planes):
    order = [p] + [p * 0] * (planes - 1)
    count = p * 0 + 1
    for step in range(1, planes):
        for other in (p - step, p + step):
            exists = jnp.logical_and(other >= 0, other < planes)
            for i in range(1, planes):
                order[i] = jnp.where(jnp.logical_and(exists, count == i), other, order[i])
            count = count + jnp.where(exists, 1, 0)
    return order


def positions(n):
    me = lax.axis_index("tile")
    p = lax.div(me, SPLIT)
    q = lax.rem(me, SPLIT)
    return me, p, lax.div(q, 2), lax.rem(q, 2), nearest_first(p, n // SPLIT)


def device(plane, yy, cc):
    return plane * SPLIT + yy * 2 + cc


def layer_kernel(
    n, rows, cap, q_ref, k_ref, v_ref, mod_ref, chooser_ref, high_ref, low_ref, first_ref, second_ref,
    out_ref, att, norm, slots, keys, vals, halo_send, halo_recv, halo_own,
    tokens, first, second, hidden, part, r1, r2, r3,
    send_sem, token_sem, s1_sem, s2_sem, s3_sem, own_sem,
):
    me, p, y, c, plane_of = positions(n)
    loads = [
        pltpu.make_async_copy(first_ref, first, own_sem.at[1]),
        pltpu.make_async_copy(second_ref, second, own_sem.at[2]),
    ]
    for load in loads:
        load.start()
    targets = [device(p, 1 - y, c), device(p, y, 1 - c)]
    targets += [device(plane, y, c) for plane in plane_of[1:]]
    pending = attention_kernel(
        n, rows, q_ref, k_ref, v_ref, mod_ref, att, norm, keys, vals, halo_send, halo_recv, halo_own,
        also=targets,
    )
    chunk = 512

    def pick(step, carry):
        cols = pl.ds(pl.multiple_of(step * chunk, chunk), chunk)
        slots[:, cols] = jnp.dot(
            chooser_ref[...], norm[:, cols], preferred_element_type=jnp.float32
        ).astype(slots.dtype)
        return carry

    lax.fori_loop(0, D // chunk, pick, 0)
    expert_part(
        n, cap, slots, att, mod_ref, high_ref, low_ref, loads, out_ref,
        tokens, first, second, hidden, part, r1, r2, r3,
        send_sem, token_sem, s1_sem, s2_sem, s3_sem, own_sem,
    )
    for copy, exists in pending:
        when(exists, copy.wait_send)


def expert_part(
    n, cap, slots_ref, att_ref, mod_ref, high_ref, low_ref, weights, out_ref,
    tokens, first, second, hidden, part, r1, r2, r3,
    send_sem, token_sem, s1_sem, s2_sem, s3_sem, own_sem,
):
    planes = n // SPLIT
    width = first.shape[1]
    me, p, y, c, plane_of = positions(n)
    beside = device(p, 1 - y, c)
    twin = device(p, y, 1 - c)

    def block(buf, index):
        return buf.at[pl.ds(pl.multiple_of(index * cap, 16), cap), :]

    mine = pltpu.make_async_copy(block(slots_ref, p), block(tokens, me), own_sem.at[0])
    mine.start()

    sends = []

    def push(src, dst, recv, target):
        copy = remote(src, dst, send_sem.at[len(sends)], recv, target)
        copy.start()
        sends.append(copy)

    def landed(dst, recv):
        remote(dst, dst, send_sem.at[0], recv, me).wait_recv()

    def give(tile, target):
        push(block(tokens, tile), block(tokens, tile), token_sem.at[tile], target)

    def take(tile):
        landed(block(tokens, tile), token_sem.at[tile])

    for target in (beside, twin):
        push(block(slots_ref, p), block(tokens, me), token_sem.at[me], target)
    for plane in plane_of[1:]:
        push(block(slots_ref, plane), block(tokens, me), token_sem.at[me], device(plane, y, c))

    def forward(i, cond=True, copies=None):
        tile = device(plane_of[i], y, c)
        if copies is None:
            copies = []
            for target in (beside, twin):
                ref = block(tokens, tile)
                copies.append(remote(ref, ref, send_sem.at[len(sends)], token_sem.at[tile], target))
                sends.append(copies[-1])

        def go():
            take(tile)
            for copy in copies:
                copy.start()

        when(cond, go)
        return copies

    def forward_more(i):
        tile = device(plane_of[i], 1 - y, c)
        take(tile)
        give(tile, twin)

    group = SPLIT * cap
    chunk = min(width, 256)
    chunk_out = 512

    def compute(i):
        plane = plane_of[i]
        for yy in (0, 1):
            take(device(plane, yy, 1 - c))
        at = pl.ds(pl.multiple_of(plane * group, 16), group)

        def one(step, carry):
            cols = pl.ds(pl.multiple_of(step * chunk, chunk), chunk)
            raw = jnp.dot(tokens[at, :], first[:, cols], preferred_element_type=jnp.float32)
            hidden[:, cols] = jax.nn.gelu(raw, approximate=True).astype(hidden.dtype)
            return carry

        lax.fori_loop(0, width // chunk, one, 0)

        def two(step, carry):
            cols = pl.ds(pl.multiple_of(step * chunk_out, chunk_out), chunk_out)
            raw = jnp.dot(hidden[...], second[:, cols], preferred_element_type=jnp.float32)
            part[at, cols] = raw.astype(part.dtype)
            return carry

        lax.fori_loop(0, D // chunk_out, two, 0)
        for yy in (0, 1):
            push(
                block(part, device(plane, yy, 1 - c)),
                block(r1, plane * 2 + yy),
                s1_sem.at[plane, yy],
                twin,
            )

    def add(tile, other, index):
        def body(step, carry):
            at = pl.ds(pl.multiple_of(tile * cap + step * 16, 16), 16)
            extra = other[pl.ds(pl.multiple_of(index * cap + step * 16, 16), 16), :]
            part[at, :] = (part[at, :].astype(jnp.float32) + extra.astype(jnp.float32)).astype(part.dtype)
            return carry

        lax.fori_loop(0, cap // 16, body, 0)

    def fold_twin(i):
        plane = plane_of[i]
        for yy in (1 - y, y):
            landed(block(r1, plane * 2 + yy), s1_sem.at[plane, yy])
            add(device(plane, yy, c), r1, plane * 2 + yy)
            if yy is not y:
                push(block(part, device(plane, yy, c)), block(r2, plane), s2_sem.at[plane], beside)

    def fold_beside(i):
        plane = plane_of[i]
        landed(block(r2, plane), s2_sem.at[plane])
        tile = device(plane, y, c)
        if i == 0:

            def body(step, carry):
                at = pl.ds(pl.multiple_of(p * cap + step * 16, 16), 16)
                own = part[pl.ds(pl.multiple_of(me * cap + step * 16, 16), 16), :]
                r3[at, :] = (own.astype(jnp.float32) + r2[at, :].astype(jnp.float32)).astype(r3.dtype)
                return carry

            lax.fori_loop(0, cap // 16, body, 0)
        else:
            add(tile, r2, plane)
            push(block(part, tile), block(r3, p), s3_sem.at[p], tile)

    mine.wait()
    take(beside)
    give(beside, twin)
    for load in weights:
        load.wait()
    inner = jnp.logical_and(p > 0, p < planes - 1)
    if planes > 1:
        forward(1)
    if planes > 2:
        early = forward(2, inner)
    compute(0)
    fold_twin(0)
    for i in range(1, planes):
        forward_more(i)
        if i >= 2 and i + 1 < planes:
            forward(i + 1)
        compute(i)
        fold_twin(i)
        fold_beside(i - 1)
        if i == 1 and planes > 2:
            forward(2, jnp.logical_not(inner), early)
    fold_beside(planes - 1)
    for plane in plane_of[1:]:
        landed(block(r3, plane), s3_sem.at[plane])

    def finish(step, carry):
        cols = pl.ds(pl.multiple_of(step * chunk_out, chunk_out), chunk_out)
        found = r3[:, cols]
        mixture = jnp.dot(high_ref[...], found, preferred_element_type=jnp.float32)
        mixture = mixture + jnp.dot(low_ref[...], found, preferred_element_type=jnp.float32)
        out_ref[:, cols] = (
            att_ref[:, cols].astype(jnp.float32) + mod_ref[2:3, cols] * mixture
        ).astype(out_ref.dtype)
        return carry

    lax.fori_loop(0, D // chunk_out, finish, 0)
    for copy in sends:
        copy.wait_send()


def kernel_bytes(n, cap, width):
    planes = n // SPLIT
    lines = 2 * n * cap + planes * 5 * cap + 2 * 3 * halo_levels(n) * cap * planes // 3
    return 2 * (lines * D + 2 * width * D)


def layer(queries, key_rows, values, modulation, expert_in, expert_out, routes, gate_fixed):
    n = lax.axis_size("tile")
    rows = queries.shape[0]
    width = expert_in.shape[1]
    planes = n // SPLIT
    cap = 3 * rows // planes
    flat = routes.reshape(-1)
    target = flat * cap + slot_table(flat, planes)
    target = target.reshape(rows, 2)
    scale = gate_fixed.astype(jnp.float32) / 1024.0
    lines = jnp.arange(planes * cap, dtype=jnp.int32)
    chooser = sum(
        (target[None, :, k] == lines[:, None]).astype(jnp.float32) for k in range(2)
    ).astype(jnp.bfloat16)
    gates = sum(
        jnp.where(target[:, k, None] == lines[None, :], scale[:, k, None], 0.0) for k in range(2)
    )
    coarse = jnp.floor(gates * 128.0) / 128.0
    high = coarse.astype(jnp.bfloat16)
    low = (gates - coarse).astype(jnp.bfloat16)
    levels = halo_levels(n)
    tiles = 3 * levels
    vmem = pl.BlockSpec(memory_space=pltpu.VMEM)
    hbm = pl.BlockSpec(memory_space=pl.ANY)
    dma = pltpu.SemaphoreType.DMA
    count_sends = 8 * planes + 8
    bf = jnp.bfloat16
    return pl.pallas_call(
        functools.partial(layer_kernel, n, rows, cap),
        name="whole_layer",
        out_shape=jax.ShapeDtypeStruct((rows, D), bf),
        in_specs=[vmem, hbm, hbm, vmem, vmem, vmem, vmem, hbm, hbm],
        out_specs=vmem,
        scratch_shapes=[
            pltpu.VMEM((rows, D), bf),
            pltpu.VMEM((rows, D), bf),
            pltpu.VMEM((planes * cap, D), bf),
            pltpu.VMEM((tiles * rows, D), bf),
            pltpu.VMEM((tiles * rows, D), bf),
            dma((4 * (2 + 3 * (levels - 1)),)),
            dma((tiles, 4)),
            dma((2,)),
            pltpu.VMEM((n * cap, D), bf),
            pltpu.VMEM((D, width), bf),
            pltpu.VMEM((width, D), bf),
            pltpu.VMEM((SPLIT * cap, width), bf),
            pltpu.VMEM((n * cap, D), bf),
            pltpu.VMEM((planes * 2 * cap, D), bf),
            pltpu.VMEM((planes * cap, D), bf),
            pltpu.VMEM((planes * cap, D), bf),
            dma((count_sends,)),
            dma((n,)),
            dma((planes, 2)),
            dma((planes,)),
            dma((planes,)),
            dma((3,)),
        ],
        compiler_params=pltpu.CompilerParams(
            collective_id=1, has_side_effects=True, vmem_limit_bytes=VMEM_LIMIT
        ),
    )(queries, key_rows, values, modulation, chooser, high, low, expert_in, expert_out)


def slot_table(flat, experts_count):
    onehot = (flat[:, None] == jnp.arange(experts_count, dtype=jnp.int32)[None, :]).astype(
        jnp.int32
    )
    before = jnp.cumsum(onehot, axis=0) - onehot
    return jnp.sum(before * onehot, axis=1)


def expert_apply(rows, first_weight, second_weight):
    hidden = jax.nn.gelu(
        jnp.dot(rows, first_weight, preferred_element_type=jnp.float32), approximate=True
    ).astype(jnp.bfloat16)
    return jnp.dot(hidden, second_weight, preferred_element_type=jnp.float32).astype(jnp.bfloat16)


def experts_sparse(normed, attended, modulation, expert_in, expert_out, routes, gate_fixed):
    devices = lax.axis_size("tile")
    rows_dev = normed.shape[0]
    experts_count = devices // SPLIT
    capacity = 3 * rows_dev // experts_count
    flat = routes.reshape(-1)
    slots = slot_table(flat, experts_count)
    target = flat * capacity + slots
    chooser = (
        target[None, :] == jnp.arange(experts_count * capacity, dtype=jnp.int32)[:, None]
    ).astype(jnp.bfloat16)
    chooser = chooser.reshape(experts_count * capacity, rows_dev, 2).sum(axis=2)
    buffer = jnp.dot(chooser, normed, preferred_element_type=jnp.float32).astype(jnp.bfloat16)
    copies = jnp.broadcast_to(
        buffer.reshape(experts_count, 1, capacity, D), (experts_count, SPLIT, capacity, D)
    ).reshape(devices, capacity, D)
    received = lax.all_to_all(copies, "tile", split_axis=0, concat_axis=0, tiled=True)
    sources = received.shape[0]
    count = received.shape[1]
    partial_value = expert_apply(received.reshape(sources * count, D), expert_in, expert_out)
    returned = lax.all_to_all(
        partial_value.reshape(sources, count, D), "tile", split_axis=0, concat_axis=0, tiled=True
    )
    summed = jnp.sum(
        returned.reshape(experts_count, SPLIT, capacity, D).astype(jnp.float32), axis=1
    )
    expert_rows = summed.astype(jnp.bfloat16).reshape(experts_count * capacity, D)
    picked = jnp.take(expert_rows, target, axis=0).reshape(rows_dev, 2, D)
    gate_scale = gate_fixed.astype(jnp.float32) / 1024.0
    mixture = jnp.sum(picked.astype(jnp.float32) * gate_scale[:, :, None], axis=1)
    return (attended.astype(jnp.float32) + modulation[2] * mixture).astype(jnp.bfloat16)


def shards(queries, key_rows, values, modulation, expert_in, expert_out, routes, gate_fixed):
    n = lax.axis_size("tile")
    cap = 3 * queries.shape[0] // (n // SPLIT)
    if cap % 16 == 0 and kernel_bytes(n, cap, expert_in.shape[1]) < VMEM_LIMIT * 3 // 4:
        return layer(queries, key_rows, values, modulation, expert_in, expert_out, routes, gate_fixed)
    attended, normed = attention(queries, key_rows, values, modulation)
    return experts_sparse(normed, attended, modulation, expert_in, expert_out, routes, gate_fixed)


def solution(mesh):
    placed = (
        P(("groups", "tile"), None),
        P(("groups", "tile"), None),
        P(("groups", "tile"), None),
        P("groups", None),
        P(None, "tile"),
        P("tile", None),
        P(("groups", "tile"), None),
        P(("groups", "tile"), None),
    )
    return jax.shard_map(
        shards, mesh=mesh, in_specs=placed, out_specs=P(("groups", "tile"), None), check_vma=False
    )
```
